256 devices in a mesh: region: 16 (over y, z_hi), dev: 16 (over x, z_lo, core).
Axes of the slice: x: 4, y: 4, z: 8 (z_hi: 4, z_lo: 2; z = z_hi * 2 + z_lo), core: 2. Of those that a mesh axis runs over, the one named last changes fastest.
Arguments:
- interior: float32 [16, 16, 384, 384], P('region', 'dev'), may hold values from -6.5 to 8.5, as said below
- coupling: float32 [16, 16, 384, 640], P('region', 'dev'), may hold values from -1 to 1
- tile_mask: int32 [16, 16, 5], P('region', 'dev'), may hold values 0 or 1
- prior: float32 [16, 640, 640], P('region', 'dev'), may hold values from -3.5 to 6, as said below
- sep_map: int32 [16, 384], P('region'), may hold values from 0 to 383, each once within a row
- nat_diag: float32 [384], replicated, may hold values from 0.25 to 2.5
Outputs:
- interior_cov: float32 [16, 16, 384, 384], P('region', 'dev')
- regional_cov: float32 [16, 640, 640], P('region', 'dev')
The draws below stay inside these ranges and needn't reach their ends.
Inputs may be any that keep to these rules, and one draw needn't show every extreme that they name: `interior`: symmetric positive definite, smallest eigenvalue 0.5 or more. `prior`: symmetric positive definite. `sep_map`: each region's row names every national separator once.
All inputs are finite; a program needn't handle non-finite values. No bound on the sum of `tile_mask` on one device may be relied on, other than what follows from the above.
Results may differ from the reference program's by a relative error of at most 0.00011.
Values sent between devices are 32-bit elements; how exact they have to be, the bound alone decides.
A program may use at most 64 MiB of HBM per device.

```python
import math
import jax
import jax.numpy as jnp
from jax import lax

NI = 384
ELIMINATED_COUNT = 256
NS = 384
TILE = 128
NRC = 640
TILES = 5
NR = 16
ND = 16


def sym_block(key, lead, order, strength, low, high):
    first, second = jax.random.split(key)
    raw = jnp.clip(jax.random.normal(first, lead + (order, order), jnp.float32), -4.0, 4.0)
    norms = jnp.sqrt(jnp.sum(raw * raw, axis=-1, keepdims=True)) + 1e-06
    rows_unit = raw * (jnp.sqrt(jnp.float32(order)) / norms)
    gram = jnp.einsum('...ik,...jk->...ij', rows_unit, rows_unit) / jnp.float32(order)
    gram = 0.5 * (gram + jnp.swapaxes(gram, -1, -2))
    ident = jnp.eye(order, dtype=jnp.float32)
    lift = jax.random.uniform(second, lead + (order,), jnp.float32, low, high)
    return strength * gram + ident * lift[..., None]


def column_scale():
    small = 1.0 / jnp.sqrt(jnp.float32(NR))
    return jnp.where(jnp.arange(NRC) < ELIMINATED_COUNT, jnp.float32(1.0), small)


def draw_interior(key, part):
    return sym_block(jax.random.fold_in(key, 11), (NR, ND), NI, 6.0, 0.5, 2.0)


def draw_prior(key, part):
    base = sym_block(jax.random.fold_in(key, 23), (NR,), NRC, 3.0, 1.5, 2.5)
    scale = column_scale()
    return base * scale[:, None] * scale[None, :]


def draw_coupling(key, part):
    inner = jax.random.fold_in(key, 37)
    shape = (NR, ND, NI, NRC)
    raw = jnp.clip(jax.random.normal(inner, shape, jnp.float32), -4.0, 4.0)
    spread = jnp.sqrt(jnp.float32(0.53) / jnp.float32(ND * NI))
    return raw * spread * column_scale()


def plant(drawn, key, low, top_value):
    longest = drawn.shape.index(max(drawn.shape))
    spots = []
    for shift in (0, 1):
        where = [jax.random.randint(jax.random.fold_in(key, axis), (), 0, length) for axis, length in enumerate(drawn.shape)]
        where[longest] = (where[longest] + shift) % drawn.shape[longest]
        spots.append(tuple(where))
    return drawn.at[spots[0]].set(low).at[spots[1]].set(top_value)


def setup_inputs(seed: int = 0) -> dict:
    splits = jax.random.split(jax.random.key(seed), 7)
    return {
        "interior": draw_interior(jax.random.fold_in(splits[6], 71), 0),
        "coupling": draw_coupling(jax.random.fold_in(splits[6], 71), 0),
        "tile_mask": plant((jax.random.randint(splits[2], (NR, ND, TILES), 0, 4) < 3).astype(jnp.int32), jax.random.fold_in(splits[2], 1), 0, 1),
        "prior": draw_prior(jax.random.fold_in(splits[6], 71), 0),
        "sep_map": jax.vmap(lambda own: jax.random.permutation(own, NS))(jax.random.split(splits[4], NR)).reshape((NR, NS)).astype(jnp.int32),
        "nat_diag": jnp.clip(jnp.exp(jax.random.uniform(splits[5], (NS,), jnp.float32, math.log(0.25), math.log(2.5))), 0.25, 2.5),
    }


FULL_PRECISION = lax.Precision.HIGHEST

def lower_solve(chol, right):
    return lax.linalg.triangular_solve(chol, right, left_side=True, lower=True, transpose_a=False)

def upper_solve(chol, right):
    return lax.linalg.triangular_solve(chol, right, left_side=True, lower=True, transpose_a=True)

def chol_apply(chol, right):
    return upper_solve(chol, lower_solve(chol, right))

def masked_block(coupling_block, mask_row):
    scale = jnp.repeat(mask_row.astype(jnp.float32), TILE)
    return coupling_block * scale[None, :]

def solved_block(interior_block, coupling_block, mask_row):
    chol = jnp.linalg.cholesky(interior_block)
    solved = lower_solve(chol, masked_block(coupling_block, mask_row))
    return (chol, solved)

def region_schur(interior_r, coupling_r, mask_r, prior_r):

    def add_term(total, items):
        chol, solved = solved_block(items[0], items[1], items[2])
        term = lax.dot_general(solved.astype(jnp.float32), solved.astype(jnp.float32), (((0,), (0,)), ((), ())), precision=FULL_PRECISION, preferred_element_type=jnp.float32)
        return (total + term, None)
    start = jnp.zeros((NRC, NRC), jnp.float32)
    summed, unused = lax.scan(add_term, start, (interior_r, coupling_r, mask_r))
    return prior_r - summed

def eliminate(complement_matrix):
    eliminated_rows = complement_matrix[:ELIMINATED_COUNT, :ELIMINATED_COUNT]
    cross = complement_matrix[:ELIMINATED_COUNT, ELIMINATED_COUNT:]
    sep_block = complement_matrix[ELIMINATED_COUNT:, ELIMINATED_COUNT:]
    eliminated_factor = jnp.linalg.cholesky(eliminated_rows)
    weight_matrix = chol_apply(eliminated_factor, cross)
    reduced = sep_block - lax.dot_general(cross.astype(jnp.float32), weight_matrix.astype(jnp.float32), (((0,), (0,)), ((), ())), precision=FULL_PRECISION, preferred_element_type=jnp.float32)
    return (eliminated_factor, weight_matrix, reduced)

def national_part(items):
    interior_r, coupling_r, mask_r, prior_r, sep_r = items
    complement_matrix = region_schur(interior_r, coupling_r, mask_r, prior_r)
    eliminated_factor, weight_matrix, reduced = eliminate(complement_matrix)
    placed = jnp.zeros((NS, NS), jnp.float32)
    return placed.at[sep_r[:, None], sep_r[None, :]].add(reduced)

def region_cov(items, cov_nat):
    interior_r, coupling_r, mask_r, prior_r, sep_r = items
    complement_matrix = region_schur(interior_r, coupling_r, mask_r, prior_r)
    eliminated_factor, weight_matrix, reduced = eliminate(complement_matrix)
    cov_sep = jnp.take(jnp.take(cov_nat, sep_r, axis=0), sep_r, axis=1)
    cross_covariance = -jnp.dot(weight_matrix.astype(jnp.float32), cov_sep.astype(jnp.float32), precision=FULL_PRECISION, preferred_element_type=jnp.float32)
    eliminated_inverse = chol_apply(eliminated_factor, jnp.eye(ELIMINATED_COUNT, dtype=jnp.float32))
    eliminated_covariance = eliminated_inverse - lax.dot_general(cross_covariance.astype(jnp.float32), weight_matrix.astype(jnp.float32), (((1,), (1,)), ((), ())), precision=FULL_PRECISION, preferred_element_type=jnp.float32)
    upper_rows = jnp.concatenate([eliminated_covariance, cross_covariance], axis=1)
    bottom = jnp.concatenate([cross_covariance.T, cov_sep], axis=1)
    cov_full = jnp.concatenate([upper_rows, bottom], axis=0)

    def one_interior(blocks):
        chol, solved = solved_block(blocks[0], blocks[1], blocks[2])
        middle = jnp.dot(solved.astype(jnp.float32), cov_full.astype(jnp.float32), precision=FULL_PRECISION, preferred_element_type=jnp.float32)
        inner = jnp.eye(NI, dtype=jnp.float32) + lax.dot_general(middle.astype(jnp.float32), solved.astype(jnp.float32), (((1,), (1,)), ((), ())), precision=FULL_PRECISION, preferred_element_type=jnp.float32)
        left = upper_solve(chol, inner)
        return upper_solve(chol, left.T)
    covs = lax.map(one_interior, (interior_r, coupling_r, mask_r))
    return (covs, cov_full)

def reference(interior, coupling, tile_mask, prior, sep_map, nat_diag):
    items = (interior, coupling, tile_mask, prior, sep_map)
    parts = lax.map(national_part, items)
    total = jnp.zeros((NS, NS), jnp.float32)
    for region in range(NR):
        total = total + parts[region]
    normal_mat = total + jnp.diag(nat_diag)
    chol_n = jnp.linalg.cholesky(normal_mat)
    cov_nat = chol_apply(chol_n, jnp.eye(NS, dtype=jnp.float32))
    interior_cov, regional_cov = lax.map(lambda group: region_cov(group, cov_nat), items)
    return (interior_cov, regional_cov)
```

```python
import functools

import jax
import jax.numpy as jnp
from jax import lax
from jax.experimental import pallas as pl
from jax.experimental.pallas import tpu as pltpu
from jax.sharding import PartitionSpec as P

NI = 384
NE = 256
NS = 384
NRC = 640
TILE = 128
EXACT = lax.Precision.HIGHEST
F32 = jnp.float32
VMEM = pltpu.VMEM


def dot(a, b, dims=((1,), (0,))):
    return lax.dot_general(a, b, (dims, ((), ())), precision=EXACT, preferred_element_type=F32)


def split3(x):
    h = x.astype(jnp.bfloat16)
    rest = x - h.astype(F32)
    m = rest.astype(jnp.bfloat16)
    return h, m, (rest - m.astype(F32)).astype(jnp.bfloat16)


def select_right(x, onehot, dims=((1,), (0,))):
    h, m, l = (lax.dot_general(part, onehot, (dims, ((), ())), preferred_element_type=F32) for part in split3(x))
    return (h + m) + l


def select_left(onehot, x, dims=((1,), (0,))):
    h, m, l = (lax.dot_general(onehot, part, (dims, ((), ())), preferred_element_type=F32) for part in split3(x))
    return (h + m) + l


def row(x, k):
    return jnp.broadcast_to(x[k : k + 1, :], (8, 128))


def col(x, k):
    return jnp.broadcast_to(x[:, k : k + 1], (8, 128))


def recip(x):
    r = pl.reciprocal(x, approx=True)
    r = r * (2.0 - x * r)
    return r * (2.0 - x * r)


def inverse8(c, sub):
    c = list(c)
    for k in range(0, 8, 2):
        k1 = k + 1
        a, b, b2, e = row(c[k], k), row(c[k1], k), row(c[k], k1), row(c[k1], k1)
        rd = recip(a * e - b * b2)
        ia, ib, ib2, ie = e * rd, -(b * rd), -(b2 * rd), a * rd
        r0, r1 = sub == k, sub == k1
        ck, ck1 = c[k], c[k1]
        for j in range(8):
            if j in (k, k1):
                continue
            x, y = row(c[j], k), row(c[j], k1)
            m0, m1 = ia * x + ib * y, ib2 * x + ie * y
            c[j] = jnp.where(r0, m0, jnp.where(r1, m1, c[j] - (ck * m0 + ck1 * m1)))
        c[k] = jnp.where(r0, ia, jnp.where(r1, ib2, -(ck * ia + ck1 * ib2)))
        c[k1] = jnp.where(r0, ib, jnp.where(r1, ie, -(ck * ib + ck1 * ie)))
    return c


def sum8(t):
    return ((t[0] + t[1]) + (t[2] + t[3])) + ((t[4] + t[5]) + (t[6] + t[7]))


def inverse128(a):
    a = list(a)
    n = len(a)
    sub = lax.broadcasted_iota(jnp.int32, (8, 128), 0)
    lane = lax.broadcasted_iota(jnp.int32, (8, 128), 1)
    for p in range(n):
        lo = 8 * p
        r = a[p]
        d = inverse8([col(r, lo + j) for j in range(8)], sub)
        u = sum8([d[j] * row(r, j) for j in range(8)])
        for j in range(8):
            u = jnp.where(lane == lo + j, d[j], u)
        inside = (lane >= lo) & (lane < lo + 8)
        rows = [row(u, j) for j in range(8)]
        for step in range(n - 1):
            i = (p + 1 + step) % n
            x = a[i]
            a[i] = jnp.where(inside, 0.0, x) - sum8([col(x, lo + j) * rows[j] for j in range(8)])
        a[p] = u
    return a


def invert(w, blocks):
    def step(k, _):
        at = pl.ds(pl.multiple_of(k * TILE, TILE), TILE)
        full = w[at, at]
        pivot = jnp.concatenate(inverse128([full[8 * i : 8 * i + 8, :] for i in range(TILE // 8)]), axis=0)
        column = w[:, at]
        w[at, at] = jnp.zeros((TILE, TILE), F32)
        scaled = dot(pivot, w[at, :])
        w[:, at] = jnp.zeros((blocks * TILE, TILE), F32)
        w[...] = w[...] - dot(column, scaled)
        w[:, at] = -dot(column, pivot)
        w[at, :] = scaled
        w[at, at] = pivot
        return 0

    lax.fori_loop(0, blocks, step, 0)


def national(sep_row):
    return (lax.broadcasted_iota(jnp.int32, (NS, NS), 0) == sep_row).astype(jnp.bfloat16)


def first_kernel(mask, interior, coupling, prior, sep, own_row, ainv, gain, ec, ss):
    ainv[...] = interior[...]
    invert(ainv, NI // TILE)
    perm = national(sep[...])
    m_e = jnp.concatenate([coupling[:, TILE * t : TILE * (t + 1)] * mask[0, t].astype(F32) for t in range(2)], axis=1)
    m_s = jnp.concatenate([coupling[:, TILE * t : TILE * (t + 1)] * mask[0, t].astype(F32) for t in range(2, 5)], axis=1)
    m_s = select_right(m_s, perm, ((1,), (1,)))
    g_e = dot(ainv[...], m_e)
    g_s = dot(ainv[...], m_s)
    gain[:, :NE] = g_e
    gain[:, NE:] = g_s
    place = (lax.broadcasted_iota(jnp.int32, (NRC, own_row.shape[1]), 0) == own_row[...]).astype(jnp.bfloat16)
    p_s = select_right(prior[:, NE:], perm, ((1,), (1,)))
    ec[:, :NE] = select_left(place[:NE], prior[:, :NE]) - dot(m_e, g_e, ((0,), (0,)))
    ec[:, NE:] = select_left(place[:NE], p_s) - dot(m_e, g_s, ((0,), (0,)))
    ss[...] = select_left(place[NE:], p_s) - dot(m_s, g_s, ((0,), (0,)))


def second_kernel(ec, ss_own, own24, einv, weights, reduced_own):
    einv[...] = ec[:, :NE]
    invert(einv, NE // TILE)
    cross = ec[:, NE:]
    w = dot(einv[...], cross)
    weights[...] = w
    pick = (lax.broadcasted_iota(jnp.int32, (ss_own.shape[0], NS), 1) == own24[...]).astype(jnp.bfloat16)
    reduced_own[...] = ss_own[...] - dot(select_left(pick, cross, ((1,), (1,))), w)


def third_kernel(total, diag, sep, own_col, ainv, gain, einv, weights, out, rows, normal, h):
    i0 = lax.broadcasted_iota(jnp.int32, (NS, NS), 0)
    i1 = lax.broadcasted_iota(jnp.int32, (NS, NS), 1)
    normal[...] = total[...] + jnp.where(i0 == i1, diag[...], 0.0)
    invert(normal, NS // TILE)
    x = normal[...]
    w = weights[...]
    g_e = gain[:, :NE]
    h[...] = gain[:, NE:] - dot(g_e, w)
    base = ainv[...] + dot(dot(g_e, einv[...]), g_e, ((1,), (1,)))
    out[...] = base + dot(dot(h[...], x), h[...], ((1,), (1,)))
    count = own_col.shape[0]
    pick_e = (lax.broadcasted_iota(jnp.int32, (count, NE), 1) == own_col[...]).astype(jnp.bfloat16)
    pick_s = (lax.broadcasted_iota(jnp.int32, (count, NS), 1) + NE == own_col[...]).astype(F32)
    b_rows = pick_s - select_left(pick_e, w)
    t = dot(b_rows, x)
    rows[:, :NE] = select_left(pick_e, einv[...]) - dot(t, w, ((1,), (1,)))
    rows[:, NE:] = select_right(t, national(sep[...]))


def body(interior, coupling, tile_mask, prior, sep_map, nat_diag):
    dev_count = lax.axis_size("dev")
    own = lax.axis_index("dev")
    count = NRC // dev_count
    share = NS // dev_count
    sds = lambda *shape: jax.ShapeDtypeStruct(shape, F32)
    v = pl.BlockSpec(memory_space=VMEM)
    s = pl.BlockSpec(memory_space=pltpu.SMEM)
    where = jnp.concatenate([jnp.arange(NE, dtype=jnp.int32), sep_map[0] + NE])
    own_map = lax.dynamic_slice_in_dim(where, own * count, count, 0)
    own24 = (own * share + jnp.arange(share, dtype=jnp.int32))[:, None]
    ainv, gain, ec, ss = pl.pallas_call(
        first_kernel,
        out_shape=(sds(NI, NI), sds(NI, NRC), sds(NE, NRC), sds(NS, NS)),
        in_specs=[s, v, v, v, v, v],
        out_specs=(v, v, v, v),
    )(tile_mask[0], interior[0, 0], coupling[0, 0], prior[0], sep_map, own_map[None, :])
    ec, ss = lax.psum((ec, ss), "dev")
    ss_own = lax.dynamic_slice_in_dim(ss, own * share, share, 0)
    einv, weights, reduced_own = pl.pallas_call(
        second_kernel,
        out_shape=(sds(NE, NE), sds(NE, NS), sds(share, NS)),
        in_specs=[v, v, v],
        out_specs=(v, v, v),
    )(ec, ss_own, own24)
    total = lax.all_gather(lax.psum(reduced_own, "region"), "dev", axis=0, tiled=True)
    result, rows = pl.pallas_call(
        third_kernel,
        out_shape=(sds(NI, NI), sds(count, NRC)),
        in_specs=[v] * 8,
        out_specs=(v, v),
        scratch_shapes=[VMEM((NS, NS), F32), VMEM((NI, NS), F32)],
    )(total, nat_diag[None, :], sep_map, own_map[:, None], ainv, gain, einv, weights)
    return (result[None, None], rows[None])


def solution(mesh):
    placed = (
        P("region", "dev", None, None),
        P("region", "dev", None, None),
        P("region", "dev", None),
        P("region", "dev", None),
        P("region", None),
        P(),
    )
    return jax.shard_map(
        body,
        mesh=mesh,
        in_specs=placed,
        out_specs=(P("region", "dev", None, None), P("region", "dev", None)),
        check_vma=False,
    )
```

```python
import functools

import jax
import jax.numpy as jnp
from jax import lax
from jax.experimental import pallas as pl
from jax.experimental.pallas import tpu as pltpu
from jax.sharding import PartitionSpec as P

NI = 384
NE = 256
NS = 384
NRC = 640
TILE = 128
EXACT = lax.Precision.HIGHEST
F32 = jnp.float32
VMEM = pltpu.VMEM
MESH = pl.DeviceIdType.MESH


def dot(a, b, dims=((1,), (0,))):
    return lax.dot_general(a, b, (dims, ((), ())), precision=EXACT, preferred_element_type=F32)


def split3(x):
    h = x.astype(jnp.bfloat16)
    rest = x - h.astype(F32)
    m = rest.astype(jnp.bfloat16)
    return h, m, (rest - m.astype(F32)).astype(jnp.bfloat16)


def select_right(x, onehot, dims=((1,), (0,))):
    h, m, l = (lax.dot_general(part, onehot, (dims, ((), ())), preferred_element_type=F32) for part in split3(x))
    return (h + m) + l


def select_left(onehot, x, dims=((1,), (0,))):
    h, m, l = (lax.dot_general(onehot, part, (dims, ((), ())), preferred_element_type=F32) for part in split3(x))
    return (h + m) + l


def row(x, k):
    return jnp.broadcast_to(x[k : k + 1, :], (8, 128))


def col(x, k):
    return jnp.broadcast_to(x[:, k : k + 1], (8, 128))


def recip(x):
    r = pl.reciprocal(x, approx=True)
    r = r * (2.0 - x * r)
    return r * (2.0 - x * r)


def inverse8(c, sub):
    c = list(c)
    for k in range(0, 8, 2):
        k1 = k + 1
        a, b, b2, e = row(c[k], k), row(c[k1], k), row(c[k], k1), row(c[k1], k1)
        rd = recip(a * e - b * b2)
        ia, ib, ib2, ie = e * rd, -(b * rd), -(b2 * rd), a * rd
        r0, r1 = sub == k, sub == k1
        ck, ck1 = c[k], c[k1]
        for j in range(8):
            if j in (k, k1):
                continue
            x, y = row(c[j], k), row(c[j], k1)
            m0, m1 = ia * x + ib * y, ib2 * x + ie * y
            c[j] = jnp.where(r0, m0, jnp.where(r1, m1, c[j] - (ck * m0 + ck1 * m1)))
        c[k] = jnp.where(r0, ia, jnp.where(r1, ib2, -(ck * ia + ck1 * ib2)))
        c[k1] = jnp.where(r0, ib, jnp.where(r1, ie, -(ck * ib + ck1 * ie)))
    return c


def sum8(t):
    return ((t[0] + t[1]) + (t[2] + t[3])) + ((t[4] + t[5]) + (t[6] + t[7]))


def inverse128(a):
    a = list(a)
    n = len(a)
    sub = lax.broadcasted_iota(jnp.int32, (8, 128), 0)
    lane = lax.broadcasted_iota(jnp.int32, (8, 128), 1)
    for p in range(n):
        lo = 8 * p
        r = a[p]
        d = inverse8([col(r, lo + j) for j in range(8)], sub)
        u = sum8([d[j] * row(r, j) for j in range(8)])
        for j in range(8):
            u = jnp.where(lane == lo + j, d[j], u)
        inside = (lane >= lo) & (lane < lo + 8)
        rows = [row(u, j) for j in range(8)]
        for step in range(n - 1):
            i = (p + 1 + step) % n
            x = a[i]
            a[i] = jnp.where(inside, 0.0, x) - sum8([col(x, lo + j) * rows[j] for j in range(8)])
        a[p] = u
    return a


def invert(w, blocks):
    def step(k, _):
        at = pl.ds(pl.multiple_of(k * TILE, TILE), TILE)
        full = w[at, at]
        pivot = jnp.concatenate(inverse128([full[8 * i : 8 * i + 8, :] for i in range(TILE // 8)]), axis=0)
        column = w[:, at]
        w[at, at] = jnp.zeros((TILE, TILE), F32)
        scaled = dot(pivot, w[at, :])
        w[:, at] = jnp.zeros((blocks * TILE, TILE), F32)
        w[...] = w[...] - dot(column, scaled)
        w[:, at] = -dot(column, pivot)
        w[at, :] = scaled
        w[at, at] = pivot
        return 0

    lax.fori_loop(0, blocks, step, 0)


def national(sep_row):
    return (lax.broadcasted_iota(jnp.int32, (NS, NS), 0) == sep_row).astype(jnp.bfloat16)


def first_kernel(mask, interior, coupling, prior, sep, own_row, ainv, gain, ec, ss):
    ainv[...] = interior[...]
    invert(ainv, NI // TILE)
    perm = national(sep[...])
    m_e = jnp.concatenate([coupling[:, TILE * t : TILE * (t + 1)] * mask[0, t].astype(F32) for t in range(2)], axis=1)
    m_s = jnp.concatenate([coupling[:, TILE * t : TILE * (t + 1)] * mask[0, t].astype(F32) for t in range(2, 5)], axis=1)
    m_s = select_right(m_s, perm, ((1,), (1,)))
    g_e = dot(ainv[...], m_e)
    g_s = dot(ainv[...], m_s)
    gain[:, :NE] = g_e
    gain[:, NE:] = g_s
    place = (lax.broadcasted_iota(jnp.int32, (NRC, own_row.shape[1]), 0) == own_row[...]).astype(jnp.bfloat16)
    p_s = select_right(prior[:, NE:], perm, ((1,), (1,)))
    ec[:, :NE] = select_left(place[:NE], prior[:, :NE]) - dot(m_e, g_e, ((0,), (0,)))
    ec[:, NE:] = select_left(place[:NE], p_s) - dot(m_e, g_s, ((0,), (0,)))
    ss[...] = select_left(place[NE:], p_s) - dot(m_s, g_s, ((0,), (0,)))


def second_kernel(
    ec, ss, ainv, gain, own24, total, einv, weights, base, h,
    half_e, half_x, half_s, acc_e, acc_x, acc_s, rs_e, rs_x, rs_s, e_all, x_all, y_all, z_all, n_all,
    half_sem, rs_sem, ag_sem, reg_sem, send_sem,
):
    me, region = lax.axis_index("dev"), lax.axis_index("region")
    q, core = lax.div(me, 2), lax.rem(me, 2)
    y, z = lax.div(region, 4), lax.rem(region, 4)
    place = core * 8 + q
    sent = []

    def send(src, dst, recv, **where):
        copy = pltpu.make_async_remote_copy(
            src_ref=src, dst_ref=dst, send_sem=send_sem.at[len(sent)], recv_sem=recv,
            device_id=where, device_id_type=MESH,
        )
        copy.start()
        sent.append(copy)

    def arrived(dst, recv):
        pltpu.make_async_remote_copy(
            src_ref=dst, dst_ref=dst, send_sem=send_sem.at[0], recv_sem=recv,
            device_id={"dev": lax.rem(me + 1, 16)}, device_id_type=MESH,
        ).wait_recv()

    others = [lax.rem(me + t, 16) for t in range(1, 16)]
    same_core = [lax.rem(q + t, 8) for t in range(1, 8)]
    y_peers = [lax.rem(y + t, 4) for t in range(1, 4)]
    z_peers = [lax.rem(z + t, 4) for t in range(1, 4)]

    barrier = pltpu.get_barrier_semaphore()
    for other in others:
        pl.semaphore_signal(barrier, inc=1, device_id={"dev": other}, device_id_type=MESH)
    for other in y_peers:
        pl.semaphore_signal(barrier, inc=1, device_id={"region": other * 4 + z}, device_id_type=MESH)
    for other in z_peers:
        pl.semaphore_signal(barrier, inc=1, device_id={"region": y * 4 + other}, device_id_type=MESH)
    pl.semaphore_wait(barrier, 21)

    partner = q * 2 + (1 - core)
    away, home = 1 - core, core
    ec_rows = lambda at: pl.ds(pl.multiple_of(at * 128, 128), 128)
    ss_rows = lambda at: pl.ds(pl.multiple_of(at * 192, 192), 192)
    parts = (
        (ec.at[ec_rows(away), pl.ds(0, NE)], half_e),
        (ec.at[ec_rows(away), pl.ds(NE, NS)], half_x),
        (ss.at[ss_rows(away), :], half_s),
    )
    for n, (src, dst) in enumerate(parts):
        send(src, dst, half_sem.at[n], dev=partner)

    def scatter(kind, acc, slots, size):
        for other in same_core:
            rows = pl.ds(pl.multiple_of(other * size, size), size)
            send(acc.at[rows, :], slots.at[q], rs_sem.at[kind, q], dev=other * 2 + core)

    def gathered(kind, acc, slots, size):
        value = acc[pl.ds(pl.multiple_of(q * size, size), size), :]
        for other in same_core:
            arrived(slots.at[other], rs_sem.at[kind, other])
            value = value + slots[other]
        return value

    def rows_of(dev, size):
        return pl.ds(pl.multiple_of((lax.rem(dev, 2) * 8 + lax.div(dev, 2)) * size, size), size)

    def spread(kind, full, size):
        for other in others:
            send(full.at[rows_of(me, size), :], full.at[rows_of(me, size), :], ag_sem.at[kind, me], dev=other)

    def complete(kind, full, size):
        for other in others:
            arrived(full.at[rows_of(other, size), :], ag_sem.at[kind, other])

    arrived(half_e, half_sem.at[0])
    acc_e[...] = ec[ec_rows(home), :NE] + half_e[...]
    scatter(0, acc_e, rs_e, 16)
    arrived(half_x, half_sem.at[1])
    acc_x[...] = ec[ec_rows(home), NE:] + half_x[...]
    scatter(1, acc_x, rs_x, 16)
    e_all[rows_of(me, 16), :] = gathered(0, acc_e, rs_e, 16)
    spread(0, e_all, 16)
    x_all[rows_of(me, 16), :] = gathered(1, acc_x, rs_x, 16)
    spread(1, x_all, 16)
    arrived(half_s, half_sem.at[2])
    acc_s[...] = ss[ss_rows(home), :] + half_s[...]
    scatter(2, acc_s, rs_s, 24)

    complete(0, e_all, 16)
    einv[...] = e_all[...]
    invert(einv, NE // TILE)
    complete(1, x_all, 16)
    cross = x_all[...]
    w = dot(einv[...], cross)
    weights[...] = w
    pick = (lax.broadcasted_iota(jnp.int32, (24, NS), 1) == own24[...]).astype(jnp.bfloat16)
    own = gathered(2, acc_s, rs_s, 24) - dot(select_left(pick, cross, ((1,), (1,))), w)

    y_all[y] = own
    for other in y_peers:
        send(y_all.at[y], y_all.at[y], reg_sem.at[0, y], region=other * 4 + z)
    g_e = gain[:, :NE]
    h[...] = gain[:, NE:] - dot(g_e, w)
    for other in y_peers:
        arrived(y_all.at[other], reg_sem.at[0, other])
    z_all[z] = (y_all[0] + y_all[1]) + (y_all[2] + y_all[3])
    for other in z_peers:
        send(z_all.at[z], z_all.at[z], reg_sem.at[1, z], region=y * 4 + other)
    base[...] = ainv[...] + dot(dot(g_e, einv[...]), g_e, ((1,), (1,)))
    for other in z_peers:
        arrived(z_all.at[other], reg_sem.at[1, other])
    n_all[rows_of(me, 24), :] = (z_all[0] + z_all[1]) + (z_all[2] + z_all[3])
    spread(2, n_all, 24)
    complete(2, n_all, 24)
    total[...] = n_all[...]
    for copy in sent:
        copy.wait_send()


def third_kernel(total, diag, sep, own_col, base, h, einv, weights, out, rows, normal):
    i0 = lax.broadcasted_iota(jnp.int32, (NS, NS), 0)
    i1 = lax.broadcasted_iota(jnp.int32, (NS, NS), 1)
    normal[...] = total[...] + jnp.where(i0 == i1, diag[...], 0.0)
    invert(normal, NS // TILE)
    x = normal[...]
    w = weights[...]
    out[...] = base[...] + dot(dot(h[...], x), h[...], ((1,), (1,)))
    count = own_col.shape[0]
    pick_e = (lax.broadcasted_iota(jnp.int32, (count, NE), 1) == own_col[...]).astype(jnp.bfloat16)
    pick_s = (lax.broadcasted_iota(jnp.int32, (count, NS), 1) + NE == own_col[...]).astype(F32)
    b_rows = pick_s - select_left(pick_e, w)
    t = dot(b_rows, x)
    rows[:, :NE] = select_left(pick_e, einv[...]) - dot(t, w, ((1,), (1,)))
    rows[:, NE:] = select_right(t, national(sep[...]))


def body(interior, coupling, tile_mask, prior, sep_map, nat_diag):
    dev_count = lax.axis_size("dev")
    own = lax.axis_index("dev")
    count = NRC // dev_count
    share = NS // dev_count
    sds = lambda *shape: jax.ShapeDtypeStruct(shape, F32)
    v = pl.BlockSpec(memory_space=VMEM)
    s = pl.BlockSpec(memory_space=pltpu.SMEM)
    where = jnp.concatenate([jnp.arange(NE, dtype=jnp.int32), sep_map[0] + NE])
    own_map = lax.dynamic_slice_in_dim(where, own * count, count, 0)
    place = (own % 2) * (dev_count // 2) + own // 2
    own24 = (place * share + jnp.arange(share, dtype=jnp.int32))[:, None]
    ainv, gain, ec, ss = pl.pallas_call(
        first_kernel,
        out_shape=(sds(NI, NI), sds(NI, NRC), sds(NE, NRC), sds(NS, NS)),
        in_specs=[s, v, v, v, v, v],
        out_specs=(v, v, v, v),
    )(tile_mask[0], interior[0, 0], coupling[0, 0], prior[0], sep_map, own_map[None, :])
    dma = pltpu.SemaphoreType.DMA
    buf = lambda *shape: VMEM(shape, F32)
    total, einv, weights, base, h = pl.pallas_call(
        second_kernel,
        out_shape=(sds(NS, NS), sds(NE, NE), sds(NE, NS), sds(NI, NI), sds(NI, NS)),
        in_specs=[v] * 5,
        out_specs=(v,) * 5,
        scratch_shapes=[
            buf(128, NE), buf(128, NS), buf(192, NS), buf(128, NE), buf(128, NS), buf(192, NS),
            buf(8, 16, NE), buf(8, 16, NS), buf(8, 24, NS), buf(NE, NE), buf(NE, NS),
            buf(4, 24, NS), buf(4, 24, NS), buf(NS, NS),
            dma((3,)), dma((3, 8)), dma((3, 16)), dma((2, 4)), dma((80,)),
        ],
        compiler_params=pltpu.CompilerParams(collective_id=0, has_side_effects=True),
    )(ec, ss, ainv, gain, own24)
    result, rows = pl.pallas_call(
        third_kernel,
        out_shape=(sds(NI, NI), sds(count, NRC)),
        in_specs=[v] * 8,
        out_specs=(v, v),
        scratch_shapes=[VMEM((NS, NS), F32)],
    )(total, nat_diag[None, :], sep_map, own_map[:, None], base, h, einv, weights)
    return (result[None, None], rows[None])


def solution(mesh):
    placed = (
        P("region", "dev", None, None),
        P("region", "dev", None, None),
        P("region", "dev", None),
        P("region", "dev", None),
        P("region", None),
        P(),
    )
    return jax.shard_map(
        body,
        mesh=mesh,
        in_specs=placed,
        out_specs=(P("region", "dev", None, None), P("region", "dev", None)),
        check_vma=False,
    )
```

```python
import jax
import jax.numpy as jnp
from jax import lax
from jax.experimental import pallas as pl
from jax.experimental.pallas import tpu as pltpu
from jax.sharding import PartitionSpec as P

NI = 384
NE = 256
NS = 384
NRC = 640
TILE = 128
EXACT = lax.Precision.HIGHEST
F32 = jnp.float32
VMEM = pltpu.VMEM
MESH = pl.DeviceIdType.MESH


def dot(a, b, dims=((1,), (0,))):
    return lax.dot_general(a, b, (dims, ((), ())), precision=EXACT, preferred_element_type=F32)


def fast(a, b, dims=((1,), (0,))):
    return lax.dot_general(a, b, (dims, ((), ())), precision=lax.Precision.HIGH, preferred_element_type=F32)


def rough(a, b):
    return lax.dot_general(
        a.astype(jnp.bfloat16), b.astype(jnp.bfloat16), (((1,), (0,)), ((), ())), preferred_element_type=F32
    )


def split3(x):
    h = x.astype(jnp.bfloat16)
    rest = x - h.astype(F32)
    m = rest.astype(jnp.bfloat16)
    return h, m, (rest - m.astype(F32)).astype(jnp.bfloat16)


def select_right(x, onehot, dims=((1,), (0,))):
    h, m, l = (lax.dot_general(part, onehot, (dims, ((), ())), preferred_element_type=F32) for part in split3(x))
    return (h + m) + l


def select_left(onehot, x, dims=((1,), (0,))):
    h, m, l = (lax.dot_general(onehot, part, (dims, ((), ())), preferred_element_type=F32) for part in split3(x))
    return (h + m) + l


def row(x, k):
    return jnp.broadcast_to(x[k : k + 1, :], (8, 128))


def col(x, k):
    return jnp.broadcast_to(x[:, k : k + 1], (8, 128))


def recip(x):
    r = pl.reciprocal(x, approx=True)
    r = r * (2.0 - x * r)
    return r * (2.0 - x * r)


def inverse8(c, sub):
    c = list(c)
    for k in range(0, 8, 2):
        k1 = k + 1
        a, b, b2, e = row(c[k], k), row(c[k1], k), row(c[k], k1), row(c[k1], k1)
        rd = recip(a * e - b * b2)
        ia, ib, ib2, ie = e * rd, -(b * rd), -(b2 * rd), a * rd
        r0, r1 = sub == k, sub == k1
        ck, ck1 = c[k], c[k1]
        for j in range(8):
            if j in (k, k1):
                continue
            x, y = row(c[j], k), row(c[j], k1)
            m0, m1 = ia * x + ib * y, ib2 * x + ie * y
            c[j] = jnp.where(r0, m0, jnp.where(r1, m1, c[j] - (ck * m0 + ck1 * m1)))
        c[k] = jnp.where(r0, ia, jnp.where(r1, ib2, -(ck * ia + ck1 * ib2)))
        c[k1] = jnp.where(r0, ib, jnp.where(r1, ie, -(ck * ib + ck1 * ie)))
    return c


def sum8(t):
    return ((t[0] + t[1]) + (t[2] + t[3])) + ((t[4] + t[5]) + (t[6] + t[7]))


def inverse128(a):
    a = list(a)
    n = len(a)
    sub = lax.broadcasted_iota(jnp.int32, (8, 128), 0)
    lane = lax.broadcasted_iota(jnp.int32, (8, 128), 1)
    for p in range(n):
        lo = 8 * p
        r = a[p]
        d = inverse8([col(r, lo + j) for j in range(8)], sub)
        u = sum8([d[j] * row(r, j) for j in range(8)])
        for j in range(8):
            u = jnp.where(lane == lo + j, d[j], u)
        inside = (lane >= lo) & (lane < lo + 8)
        rows = [row(u, j) for j in range(8)]
        for step in range(n - 1):
            i = (p + 1 + step) % n
            x = a[i]
            a[i] = jnp.where(inside, 0.0, x) - sum8([col(x, lo + j) * rows[j] for j in range(8)])
        a[p] = u
    return a


def invert(w, blocks):
    def step(k, _):
        at = pl.ds(pl.multiple_of(k * TILE, TILE), TILE)
        full = w[at, at]
        pivot = jnp.concatenate(inverse128([full[8 * i : 8 * i + 8, :] for i in range(TILE // 8)]), axis=0)
        column = w[:, at]
        w[at, at] = jnp.zeros((TILE, TILE), F32)
        scaled = dot(pivot, w[at, :])
        w[:, at] = jnp.zeros((blocks * TILE, TILE), F32)
        w[...] = w[...] - dot(column, scaled)
        w[:, at] = -dot(column, pivot)
        w[at, :] = scaled
        w[at, at] = pivot
        return 0

    lax.fori_loop(0, blocks, step, 0)


def verified_inverse(a, x, low, steps):
    n = a.shape[0]
    eye = jnp.where(
        lax.broadcasted_iota(jnp.int32, (n, n), 0) == lax.broadcasted_iota(jnp.int32, (n, n), 1), 1.0, 0.0
    )
    full = a[...]
    high = jnp.max(jnp.sum(jnp.abs(full), axis=0, keepdims=True), axis=1, keepdims=True)
    c = 2.0 / (low + high)
    rho = (high - low) / (low + high)
    scale = 2.0 / (2.0 - rho * rho)
    x[...] = (2.0 * c * scale) * eye - (c * c * scale) * full
    rho = rho * rho / (2.0 - rho * rho)
    for _ in range(steps):
        scale = 2.0 / (2.0 - rho * rho)
        now = x[...]
        x[...] = (now * 2.0 - rough(now, rough(full, now))) * scale
        rho = rho * rho / (2.0 - rho * rho)

    def more(state):
        count, size = state
        return jnp.logical_and(count < 12, jnp.logical_not(size <= 1e-3))

    def step(state):
        count, _ = state
        now = x[...]
        r = eye - fast(a[...], now)
        x[...] = now + rough(now, r)
        return count + 1, jnp.sum(r * r)

    lax.while_loop(more, step, (jnp.int32(0), jnp.float32(1.0)))
    now = x[...]
    r = eye - dot(a[...], now)
    x[...] = now + rough(now, r)

    @pl.when(jnp.logical_not(jnp.sum(r * r) <= 1e-6))
    def _():
        x[...] = a[...]
        invert(x, n // TILE)


def national(sep_row):
    return (lax.broadcasted_iota(jnp.int32, (NS, NS), 0) == sep_row).astype(jnp.bfloat16)


def first_kernel(interior, ainv):
    verified_inverse(interior, ainv, 0.5, 3)


def second_kernel(
    mask, ainv, coupling, prior, sep, total, einv, weights, base, h,
    e_own, x_own, s_own, half_e, half_x, half_s, acc_e, acc_x, acc_s, rs_e, rs_x, rs_s,
    e_all, x_all, y_all, z_all, n_all, half_sem, rs_sem, ag_sem, reg_sem, send_sem,
):
    me, region = lax.axis_index("dev"), lax.axis_index("region")
    q, core = lax.div(me, 2), lax.rem(me, 2)
    y, z = lax.div(region, 4), lax.rem(region, 4)
    sent = []

    def send(src, dst, recv, **where):
        copy = pltpu.make_async_remote_copy(
            src_ref=src, dst_ref=dst, send_sem=send_sem.at[len(sent)], recv_sem=recv,
            device_id=where, device_id_type=MESH,
        )
        copy.start()
        sent.append(copy)

    def arrived(dst, recv):
        pltpu.make_async_remote_copy(
            src_ref=dst, dst_ref=dst, send_sem=send_sem.at[0], recv_sem=recv,
            device_id={"dev": lax.rem(me + 1, 16)}, device_id_type=MESH,
        ).wait_recv()

    others = [lax.rem(me + t, 16) for t in range(1, 16)]
    same_core = [lax.rem(q + t, 8) for t in range(1, 8)]
    y_peers = [lax.rem(y + t, 4) for t in range(1, 4)]
    z_peers = [lax.rem(z + t, 4) for t in range(1, 4)]

    barrier = pltpu.get_barrier_semaphore()
    for other in others:
        pl.semaphore_signal(barrier, inc=1, device_id={"dev": other}, device_id_type=MESH)
    for other in y_peers:
        pl.semaphore_signal(barrier, inc=1, device_id={"region": other * 4 + z}, device_id_type=MESH)
    for other in z_peers:
        pl.semaphore_signal(barrier, inc=1, device_id={"region": y * 4 + other}, device_id_type=MESH)

    partner = q * 2 + (1 - core)
    away = pl.ds(pl.multiple_of((1 - core) * 64, 64), 64)
    home = pl.ds(pl.multiple_of(core * 64, 64), 64)

    def rows_of(dev):
        return pl.ds(pl.multiple_of(lax.rem(dev, 2) * 64 + lax.div(dev, 2) * 8, 8), 8)

    def halve(kind, mine, half):
        send(mine.at[away, :], half.at[:, :], half_sem.at[kind], dev=partner)

    def scatter(kind, mine, half, acc, slots):
        arrived(half, half_sem.at[kind])
        acc[...] = mine[home, :] + half[...]
        for other in same_core:
            rows = pl.ds(pl.multiple_of(other * 8, 8), 8)
            send(acc.at[rows, :], slots.at[q], rs_sem.at[kind, q], dev=other * 2 + core)

    def gathered(kind, acc, slots):
        value = acc[pl.ds(pl.multiple_of(q * 8, 8), 8), :]
        for other in same_core:
            arrived(slots.at[other], rs_sem.at[kind, other])
            value = value + slots[other]
        return value

    def spread(kind, full):
        for other in others:
            send(full.at[rows_of(me), :], full.at[rows_of(me), :], ag_sem.at[kind, me], dev=other)

    def complete(kind, full):
        for other in others:
            arrived(full.at[rows_of(other), :], ag_sem.at[kind, other])

    count = prior.shape[0]
    perm = national(sep[...])
    m_e = jnp.concatenate([coupling[:, TILE * t : TILE * (t + 1)] * mask[0, t].astype(F32) for t in range(2)], axis=1)
    g_e = fast(ainv[...], m_e)
    at = lax.broadcasted_iota(jnp.int32, (NE, count), 1) + me * count
    place_e = (lax.broadcasted_iota(jnp.int32, (NE, count), 0) == at).astype(jnp.bfloat16)
    p_e = select_left(place_e, prior[:, :NE])
    e_own[:, :TILE] = p_e[:TILE, :TILE] - dot(m_e[:, :TILE], g_e[:, :TILE], ((0,), (0,)))
    e_own[:, TILE:] = p_e[TILE:, :] - dot(m_e[:, TILE:], g_e, ((0,), (0,)))
    pl.semaphore_wait(barrier, 21)
    halve(0, e_own, half_e)

    m_s = jnp.concatenate([coupling[:, TILE * t : TILE * (t + 1)] * mask[0, t].astype(F32) for t in range(2, 5)], axis=1)
    m_s = select_right(m_s, perm, ((1,), (1,)))
    scatter(0, e_own, half_e, acc_e, rs_e)
    g_s = fast(ainv[...], m_s)
    p_s = select_right(prior[:, NE:], perm, ((1,), (1,)))
    p_x = select_left(place_e, p_s)
    x_term = dot(m_e, g_s, ((0,), (0,)))
    x_own[:, :NS] = p_x[:TILE] - x_term[:TILE]
    x_own[:, NS:] = p_x[TILE:] - x_term[TILE:]
    halve(1, x_own, half_x)
    e_all[rows_of(me), :] = gathered(0, acc_e, rs_e)
    spread(0, e_all)
    scatter(1, x_own, half_x, acc_x, rs_x)
    at = lax.broadcasted_iota(jnp.int32, (NS, count), 1) + (me * count - NE)
    local = (lax.broadcasted_iota(jnp.int32, (NS, count), 0) == at).astype(jnp.bfloat16)
    place_s = lax.dot_general(perm, local, (((1,), (0,)), ((), ())), preferred_element_type=F32).astype(jnp.bfloat16)
    p_s = select_left(place_s, p_s)
    s_own[:, :TILE] = p_s[:TILE, :TILE] - dot(m_s[:, :TILE], g_s[:, :TILE], ((0,), (0,)))
    s_own[:, TILE : 3 * TILE] = p_s[TILE:NE, :NE] - dot(m_s[:, TILE:NE], g_s[:, :NE], ((0,), (0,)))
    s_own[:, 3 * TILE :] = p_s[NE:, :] - dot(m_s[:, NE:], g_s, ((0,), (0,)))
    halve(2, s_own, half_s)
    x_all[rows_of(me), :] = gathered(1, acc_x, rs_x)
    spread(1, x_all)
    scatter(2, s_own, half_s, acc_s, rs_s)

    complete(0, e_all)
    einv[:TILE, :TILE] = e_all[:, :TILE]
    einv[TILE:, :] = e_all[:, TILE:]
    einv[:TILE, TILE:] = e_all[:, TILE:NE].T
    invert(einv, NE // TILE)
    complete(1, x_all)
    cross = jnp.concatenate([x_all[:, :NS], x_all[:, NS:]], axis=0)
    w = dot(einv[...], cross)
    weights[...] = w
    i0, i1 = (lax.broadcasted_iota(jnp.int32, (24, NS), d) for d in (0, 1))
    pick = (i1 == lax.div(i0, 8) * TILE + lax.rem(i0, 8) + core * 64 + q * 8).astype(jnp.bfloat16)
    part = dot(select_left(pick, cross, ((1,), (1,))), w)
    part = jnp.concatenate([part[:8, :TILE], part[8:16, :NE], part[16:, :]], axis=1)

    y_all[y] = gathered(2, acc_s, rs_s) - part
    for other in y_peers:
        send(y_all.at[y], y_all.at[y], reg_sem.at[0, y], region=other * 4 + z)
    h[...] = g_s - dot(g_e, w)
    for other in y_peers:
        arrived(y_all.at[other], reg_sem.at[0, other])
    z_all[z] = (y_all[0] + y_all[1]) + (y_all[2] + y_all[3])
    for other in z_peers:
        send(z_all.at[z], z_all.at[z], reg_sem.at[1, z], region=y * 4 + other)
    base[...] = ainv[...] + fast(dot(g_e, einv[...]), g_e, ((1,), (1,)))
    for other in z_peers:
        arrived(z_all.at[other], reg_sem.at[1, other])
    n_all[rows_of(me), :] = (z_all[0] + z_all[1]) + (z_all[2] + z_all[3])
    spread(2, n_all)
    complete(2, n_all)
    total[...] = n_all[...]
    for copy in sent:
        copy.wait_send()


def third_kernel(total, diag, sep, base, h, einv, weights, out, rows, normal, inverse):
    me = lax.axis_index("dev")
    t0, t1, t2 = total[:, :TILE], total[:, TILE : 3 * TILE], total[:, 3 * TILE :]
    normal[:TILE, :TILE] = t0
    normal[TILE:NE, :NE] = t1
    normal[NE:, :] = t2
    normal[:TILE, TILE:NE] = t1[:, :TILE].T
    normal[:TILE, NE:] = t2[:, :TILE].T
    normal[TILE:NE, NE:] = t2[:, TILE:NE].T
    i0, i1 = (lax.broadcasted_iota(jnp.int32, (NS, NS), d) for d in (0, 1))
    normal[...] = normal[...] + jnp.where(i0 == i1, diag[...], 0.0)
    verified_inverse(normal, inverse, 0.25, 2)
    x = inverse[...]
    w = weights[...]
    out[...] = base[...] + fast(fast(h[...], x), h[...], ((1,), (1,)))
    count = rows.shape[0]
    perm = national(sep[...])
    at = lambda n: lax.broadcasted_iota(jnp.int32, (count, n), 0) + me * count
    pick_e = (lax.broadcasted_iota(jnp.int32, (count, NE), 1) == at(NE)).astype(jnp.bfloat16)
    pick_s = (lax.broadcasted_iota(jnp.int32, (count, NS), 1) + NE == at(NS)).astype(jnp.bfloat16)
    pick_s = lax.dot_general(pick_s, perm, (((1,), (1,)), ((), ())), preferred_element_type=F32)
    t = dot(pick_s - select_left(pick_e, w), x)
    rows[:, :NE] = select_left(pick_e, einv[...]) - dot(t, w, ((1,), (1,)))
    rows[:, NE:] = select_right(t, perm)


def body(interior, coupling, tile_mask, prior, sep_map, nat_diag):
    count = prior.shape[1]
    sds = lambda *shape: jax.ShapeDtypeStruct(shape, F32)
    v = pl.BlockSpec(memory_space=VMEM)
    s = pl.BlockSpec(memory_space=pltpu.SMEM)
    dma = pltpu.SemaphoreType.DMA
    buf = lambda *shape: VMEM(shape, F32)
    ainv = pl.pallas_call(first_kernel, out_shape=sds(NI, NI), in_specs=[v], out_specs=v)(interior[0, 0])
    total, einv, weights, base, h = pl.pallas_call(
        second_kernel,
        out_shape=(sds(TILE, 2 * NS), sds(NE, NE), sds(NE, NS), sds(NI, NI), sds(NI, NS)),
        in_specs=[s, v, v, v, v],
        out_specs=(v,) * 5,
        scratch_shapes=[
            buf(TILE, NS), buf(TILE, 2 * NS), buf(TILE, 2 * NS),
            buf(64, NS), buf(64, 2 * NS), buf(64, 2 * NS),
            buf(64, NS), buf(64, 2 * NS), buf(64, 2 * NS),
            buf(8, 8, NS), buf(8, 8, 2 * NS), buf(8, 8, 2 * NS),
            buf(TILE, NS), buf(TILE, 2 * NS), buf(4, 8, 2 * NS), buf(4, 8, 2 * NS), buf(TILE, 2 * NS),
            dma((3,)), dma((3, 8)), dma((3, 16)), dma((2, 4)), dma((75,)),
        ],
        compiler_params=pltpu.CompilerParams(collective_id=0, has_side_effects=True),
    )(tile_mask[0], ainv, coupling[0, 0], prior[0], sep_map)
    result, rows = pl.pallas_call(
        third_kernel,
        out_shape=(sds(NI, NI), sds(count, NRC)),
        in_specs=[v] * 7,
        out_specs=(v, v),
        scratch_shapes=[buf(NS, NS), buf(NS, NS)],
    )(total, nat_diag[None, :], sep_map, base, h, einv, weights)
    return (result[None, None], rows[None])


def solution(mesh):
    placed = (
        P("region", "dev", None, None),
        P("region", "dev", None, None),
        P("region", "dev", None),
        P("region", "dev", None),
        P("region", None),
        P(),
    )
    return jax.shard_map(
        body,
        mesh=mesh,
        in_specs=placed,
        out_specs=(P("region", "dev", None, None), P("region", "dev", None)),
        check_vma=False,
    )
```

```python
import jax
import jax.numpy as jnp
from jax import lax
from jax.experimental import pallas as pl
from jax.experimental.pallas import tpu as pltpu
from jax.sharding import PartitionSpec as P

NI = 384
NE = 256
NS = 384
NRC = 640
TILE = 128
EXACT = lax.Precision.HIGHEST
F32 = jnp.float32
VMEM = pltpu.VMEM
GRANT = 24 * 1024 * 1024
MESH = pl.DeviceIdType.MESH


def dot(a, b, dims=((1,), (0,))):
    return lax.dot_general(a, b, (dims, ((), ())), precision=EXACT, preferred_element_type=F32)


def fast(a, b, dims=((1,), (0,))):
    return lax.dot_general(a, b, (dims, ((), ())), precision=lax.Precision.HIGH, preferred_element_type=F32)


def rough(a, b):
    return lax.dot_general(
        a.astype(jnp.bfloat16), b.astype(jnp.bfloat16), (((1,), (0,)), ((), ())), preferred_element_type=F32
    )


def split3(x):
    h = x.astype(jnp.bfloat16)
    rest = x - h.astype(F32)
    m = rest.astype(jnp.bfloat16)
    return h, m, (rest - m.astype(F32)).astype(jnp.bfloat16)


def select_right(x, onehot, dims=((1,), (0,))):
    h, m, l = (lax.dot_general(part, onehot, (dims, ((), ())), preferred_element_type=F32) for part in split3(x))
    return (h + m) + l


def select_left(onehot, x, dims=((1,), (0,))):
    h, m, l = (lax.dot_general(onehot, part, (dims, ((), ())), preferred_element_type=F32) for part in split3(x))
    return (h + m) + l


def row(x, k):
    return jnp.broadcast_to(x[k : k + 1, :], (8, 128))


def col(x, k):
    return jnp.broadcast_to(x[:, k : k + 1], (8, 128))


def recip(x):
    r = pl.reciprocal(x, approx=True)
    r = r * (2.0 - x * r)
    return r * (2.0 - x * r)


def inverse8(c, sub):
    c = list(c)
    for k in range(0, 8, 2):
        k1 = k + 1
        a, b, b2, e = row(c[k], k), row(c[k1], k), row(c[k], k1), row(c[k1], k1)
        rd = recip(a * e - b * b2)
        ia, ib, ib2, ie = e * rd, -(b * rd), -(b2 * rd), a * rd
        r0, r1 = sub == k, sub == k1
        ck, ck1 = c[k], c[k1]
        for j in range(8):
            if j in (k, k1):
                continue
            x, y = row(c[j], k), row(c[j], k1)
            m0, m1 = ia * x + ib * y, ib2 * x + ie * y
            c[j] = jnp.where(r0, m0, jnp.where(r1, m1, c[j] - (ck * m0 + ck1 * m1)))
        c[k] = jnp.where(r0, ia, jnp.where(r1, ib2, -(ck * ia + ck1 * ib2)))
        c[k1] = jnp.where(r0, ib, jnp.where(r1, ie, -(ck * ib + ck1 * ie)))
    return c


def sum8(t):
    return ((t[0] + t[1]) + (t[2] + t[3])) + ((t[4] + t[5]) + (t[6] + t[7]))


def inverse128(a):
    a = list(a)
    n = len(a)
    sub = lax.broadcasted_iota(jnp.int32, (8, 128), 0)
    lane = lax.broadcasted_iota(jnp.int32, (8, 128), 1)
    for p in range(n):
        lo = 8 * p
        r = a[p]
        d = inverse8([col(r, lo + j) for j in range(8)], sub)
        u = sum8([d[j] * row(r, j) for j in range(8)])
        for j in range(8):
            u = jnp.where(lane == lo + j, d[j], u)
        inside = (lane >= lo) & (lane < lo + 8)
        rows = [row(u, j) for j in range(8)]
        for step in range(n - 1):
            i = (p + 1 + step) % n
            x = a[i]
            a[i] = jnp.where(inside, 0.0, x) - sum8([col(x, lo + j) * rows[j] for j in range(8)])
        a[p] = u
    return a


def invert(w, blocks):
    def step(k, _):
        at = pl.ds(pl.multiple_of(k * TILE, TILE), TILE)
        full = w[at, at]
        pivot = jnp.concatenate(inverse128([full[8 * i : 8 * i + 8, :] for i in range(TILE // 8)]), axis=0)
        column = w[:, at]
        w[at, at] = jnp.zeros((TILE, TILE), F32)
        scaled = dot(pivot, w[at, :])
        w[:, at] = jnp.zeros((blocks * TILE, TILE), F32)
        w[...] = w[...] - dot(column, scaled)
        w[:, at] = -dot(column, pivot)
        w[at, :] = scaled
        w[at, at] = pivot
        return 0

    lax.fori_loop(0, blocks, step, 0)


def verified_inverse(a, x, low, steps):
    n = a.shape[0]
    eye = jnp.where(
        lax.broadcasted_iota(jnp.int32, (n, n), 0) == lax.broadcasted_iota(jnp.int32, (n, n), 1), 1.0, 0.0
    )
    full = a[...]
    high = jnp.max(jnp.sum(jnp.abs(full), axis=0, keepdims=True), axis=1, keepdims=True)
    c = 2.0 / (low + high)
    rho = (high - low) / (low + high)
    scale = 2.0 / (2.0 - rho * rho)
    x[...] = (2.0 * c * scale) * eye - (c * c * scale) * full
    rho = rho * rho / (2.0 - rho * rho)
    for _ in range(steps):
        scale = 2.0 / (2.0 - rho * rho)
        now = x[...]
        x[...] = (now * 2.0 - rough(now, rough(full, now))) * scale
        rho = rho * rho / (2.0 - rho * rho)

    def more(state):
        count, size = state
        return jnp.logical_and(count < 12, jnp.logical_not(size <= 1e-3))

    def step(state):
        count, _ = state
        now = x[...]
        r = eye - fast(a[...], now)
        x[...] = now + rough(now, r)
        return count + 1, jnp.sum(r * r)

    lax.while_loop(more, step, (jnp.int32(0), jnp.float32(1.0)))
    now = x[...]
    r = eye - dot(a[...], now)
    x[...] = now + rough(now, r)

    @pl.when(jnp.logical_not(jnp.sum(r * r) <= 1e-6))
    def _():
        x[...] = a[...]
        invert(x, n // TILE)


def national(sep_row):
    return (lax.broadcasted_iota(jnp.int32, (NS, NS), 0) == sep_row).astype(jnp.bfloat16)


def first_kernel(interior, ainv):
    verified_inverse(interior, ainv, 0.5, 4)


def second_kernel(
    mask, ainv, coupling, prior, sep, total, weights, base, h, b_rows, e_rows,
    e_own, x_own, s_own, half_x, half_s, acc_x, acc_s, rs_e, rs_x, rs_s, e_all, x_all, y_all, z_all, n_all,
    einv, tiles, e_sem, half_sem, rs_sem, ag_sem, reg_sem, send_sem,
):
    me, region = lax.axis_index("dev"), lax.axis_index("region")
    q, core = lax.div(me, 2), lax.rem(me, 2)
    y, z = lax.div(region, 4), lax.rem(region, 4)
    sent = []

    def send(src, dst, recv, **where):
        copy = pltpu.make_async_remote_copy(
            src_ref=src, dst_ref=dst, send_sem=send_sem.at[len(sent)], recv_sem=recv,
            device_id=where, device_id_type=MESH,
        )
        copy.start()
        sent.append(copy)

    def arrived(dst, recv):
        pltpu.make_async_remote_copy(
            src_ref=dst, dst_ref=dst, send_sem=send_sem.at[0], recv_sem=recv,
            device_id={"dev": lax.rem(me + 1, 16)}, device_id_type=MESH,
        ).wait_recv()

    others = [lax.rem(me + t, 16) for t in range(1, 16)]
    same_core = [lax.rem(q + t, 8) for t in range(1, 8)]
    y_peers = [lax.rem(y + t, 4) for t in range(1, 4)]
    z_peers = [lax.rem(z + t, 4) for t in range(1, 4)]

    barrier = pltpu.get_barrier_semaphore()
    for other in others:
        pl.semaphore_signal(barrier, inc=1, device_id={"dev": other}, device_id_type=MESH)
    for other in y_peers:
        pl.semaphore_signal(barrier, inc=1, device_id={"region": other * 4 + z}, device_id_type=MESH)
    for other in z_peers:
        pl.semaphore_signal(barrier, inc=1, device_id={"region": y * 4 + other}, device_id_type=MESH)

    partner = q * 2 + (1 - core)
    away = pl.ds(pl.multiple_of((1 - core) * 64, 64), 64)
    home = pl.ds(pl.multiple_of(core * 64, 64), 64)

    def rows_of(dev):
        return pl.ds(pl.multiple_of(lax.rem(dev, 2) * 64 + lax.div(dev, 2) * 8, 8), 8)

    def halve(kind, mine, half):
        send(mine.at[away, :], half.at[:, :], half_sem.at[kind], dev=partner)

    def scatter(kind, mine, half, acc, slots):
        arrived(half, half_sem.at[kind])
        acc[...] = mine[home, :] + half[...]
        for other in same_core:
            rows = pl.ds(pl.multiple_of(other * 8, 8), 8)
            send(acc.at[rows, :], slots.at[q], rs_sem.at[kind, q], dev=other * 2 + core)

    def gathered(kind, acc, slots):
        value = acc[pl.ds(pl.multiple_of(q * 8, 8), 8), :]
        for other in same_core:
            arrived(slots.at[other], rs_sem.at[kind, other])
            value = value + slots[other]
        return value

    def spread(kind, full):
        for other in others:
            send(full.at[rows_of(me), :], full.at[rows_of(me), :], ag_sem.at[kind, me], dev=other)

    def complete(kind, full):
        for other in others:
            arrived(full.at[rows_of(other), :], ag_sem.at[kind, other])

    count = prior.shape[0]
    perm = national(sep[...])
    m_e = jnp.concatenate([coupling[:, TILE * t : TILE * (t + 1)] * mask[0, t].astype(F32) for t in range(2)], axis=1)
    g_e = fast(ainv[...], m_e)
    at = lax.broadcasted_iota(jnp.int32, (NE, count), 1) + me * count
    place_e = (lax.broadcasted_iota(jnp.int32, (NE, count), 0) == at).astype(jnp.bfloat16)
    p_e = select_left(place_e, prior[:, :NE])
    e_own[:, :TILE] = p_e[:TILE, :TILE] - dot(m_e[:, :TILE], g_e[:, :TILE], ((0,), (0,)))
    e_own[:, TILE:] = p_e[TILE:, :] - dot(m_e[:, TILE:], g_e, ((0,), (0,)))
    pl.semaphore_wait(barrier, 21)
    for other in others:
        send(e_own.at[rows_of(other), :], rs_e.at[me], e_sem.at[me], dev=other)

    m_s = jnp.concatenate([coupling[:, TILE * t : TILE * (t + 1)] * mask[0, t].astype(F32) for t in range(2, 5)], axis=1)
    m_s = select_right(m_s, perm, ((1,), (1,)))
    g_s = fast(ainv[...], m_s)
    p_s = select_right(prior[:, NE:], perm, ((1,), (1,)))
    p_x = select_left(place_e, p_s)
    x_term = dot(m_e, g_s, ((0,), (0,)))
    x_own[:, :NS] = p_x[:TILE] - x_term[:TILE]
    x_own[:, NS:] = p_x[TILE:] - x_term[TILE:]
    halve(0, x_own, half_x)
    at = lax.broadcasted_iota(jnp.int32, (NS, count), 1) + (me * count - NE)
    local = (lax.broadcasted_iota(jnp.int32, (NS, count), 0) == at).astype(jnp.bfloat16)
    place_s = lax.dot_general(perm, local, (((1,), (0,)), ((), ())), preferred_element_type=F32).astype(jnp.bfloat16)
    p_s = select_left(place_s, p_s)
    s_own[:, :TILE] = p_s[:TILE, :TILE] - dot(m_s[:, :TILE], g_s[:, :TILE], ((0,), (0,)))
    s_own[:, TILE : 3 * TILE] = p_s[TILE:NE, :NE] - dot(m_s[:, TILE:NE], g_s[:, :NE], ((0,), (0,)))
    s_own[:, 3 * TILE :] = p_s[NE:, :] - dot(m_s[:, NE:], g_s, ((0,), (0,)))
    halve(1, s_own, half_s)

    value = e_own[rows_of(me), :]
    for other in others:
        arrived(rs_e.at[other], e_sem.at[other])
        value = value + rs_e[other]
    e_all[rows_of(me), :] = value
    spread(0, e_all)
    scatter(0, x_own, half_x, acc_x, rs_x)
    x_all[rows_of(me), :] = gathered(0, acc_x, rs_x)
    spread(1, x_all)
    scatter(1, s_own, half_s, acc_s, rs_s)

    complete(0, e_all)
    tiles[0] = e_all[:, :TILE]

    def pivot(k, _):
        block = tiles[k]
        tiles[k] = jnp.concatenate(inverse128([block[8 * i : 8 * i + 8, :] for i in range(TILE // 8)]), axis=0)

        @pl.when(k == 0)
        def _():
            tiles[2] = dot(e_all[:, TILE:NE], tiles[0])
            tiles[1] = e_all[:, NE:] - dot(tiles[2], e_all[:, TILE:NE], ((1,), (1,)))

        return 0

    lax.fori_loop(0, 2, pivot, 0)
    lower = dot(tiles[1], tiles[2])
    einv[:TILE, :TILE] = tiles[0] + dot(tiles[2], lower, ((0,), (0,)))
    einv[TILE:, :TILE] = -lower
    einv[:TILE, TILE:] = -lower.T
    einv[TILE:, TILE:] = tiles[1]
    complete(1, x_all)
    cross = jnp.concatenate([x_all[:, :NS], x_all[:, NS:]], axis=0)
    w = dot(einv[...], cross)
    weights[...] = w
    i0, i1 = (lax.broadcasted_iota(jnp.int32, (24, NS), d) for d in (0, 1))
    pick = (i1 == lax.div(i0, 8) * TILE + lax.rem(i0, 8) + core * 64 + q * 8).astype(jnp.bfloat16)
    part = dot(select_left(pick, cross, ((1,), (1,))), w)
    part = jnp.concatenate([part[:8, :TILE], part[8:16, :NE], part[16:, :]], axis=1)

    y_all[y] = gathered(1, acc_s, rs_s) - part
    for other in y_peers:
        send(y_all.at[y], y_all.at[y], reg_sem.at[0, y], region=other * 4 + z)
    h[...] = g_s - dot(g_e, w)
    for other in y_peers:
        arrived(y_all.at[other], reg_sem.at[0, other])
    z_all[z] = (y_all[0] + y_all[1]) + (y_all[2] + y_all[3])
    for other in z_peers:
        send(z_all.at[z], z_all.at[z], reg_sem.at[1, z], region=y * 4 + other)
    base[...] = ainv[...] + fast(dot(g_e, einv[...]), g_e, ((1,), (1,)))
    for other in z_peers:
        arrived(z_all.at[other], reg_sem.at[1, other])
    n_all[rows_of(me), :] = (z_all[0] + z_all[1]) + (z_all[2] + z_all[3])
    spread(2, n_all)
    at = lambda n: lax.broadcasted_iota(jnp.int32, (count, n), 0) + me * count
    pick_e = (lax.broadcasted_iota(jnp.int32, (count, NE), 1) == at(NE)).astype(jnp.bfloat16)
    pick_s = (lax.broadcasted_iota(jnp.int32, (count, NS), 1) + NE == at(NS)).astype(jnp.bfloat16)
    pick_s = lax.dot_general(pick_s, perm, (((1,), (1,)), ((), ())), preferred_element_type=F32)
    b_rows[...] = pick_s - select_left(pick_e, w)
    e_rows[...] = select_left(pick_e, einv[...])
    complete(2, n_all)
    total[...] = n_all[...]
    for copy in sent:
        copy.wait_send()


def third_kernel(total, diag, sep, base, h, weights, b_rows, e_rows, out, rows, normal, inverse):
    t0, t1, t2 = total[:, :TILE], total[:, TILE : 3 * TILE], total[:, 3 * TILE :]
    normal[:TILE, :TILE] = t0
    normal[TILE:NE, :NE] = t1
    normal[NE:, :] = t2
    normal[:TILE, TILE:NE] = t1[:, :TILE].T
    normal[:TILE, NE:] = t2[:, :TILE].T
    normal[TILE:NE, NE:] = t2[:, TILE:NE].T
    i0, i1 = (lax.broadcasted_iota(jnp.int32, (NS, NS), d) for d in (0, 1))
    normal[...] = normal[...] + jnp.where(i0 == i1, diag[...].reshape(1, NS), 0.0)
    verified_inverse(normal, inverse, 0.25, 3)
    x = inverse[...]
    w = weights[...]
    out[...] = base[...] + fast(fast(h[...], x), h[...], ((1,), (1,)))
    t = fast(b_rows[...], x)
    rows[:, :NE] = e_rows[...] - fast(t, w, ((1,), (1,)))
    rows[:, NE:] = select_right(t, national(sep[...]))


def body(interior, coupling, tile_mask, prior, sep_map, nat_diag):
    count = prior.shape[1]
    sds = lambda *shape: jax.ShapeDtypeStruct(shape, F32)
    v = pl.BlockSpec(memory_space=VMEM)
    s = pl.BlockSpec(memory_space=pltpu.SMEM)
    dma = pltpu.SemaphoreType.DMA
    buf = lambda *shape: VMEM(shape, F32)
    ainv = pl.pallas_call(
        first_kernel,
        out_shape=sds(NI, NI),
        in_specs=[v],
        out_specs=v,
        compiler_params=pltpu.CompilerParams(vmem_limit_bytes=GRANT),
    )(interior[0, 0])
    total, weights, base, h, b_rows, e_rows = pl.pallas_call(
        second_kernel,
        out_shape=(sds(TILE, 2 * NS), sds(NE, NS), sds(NI, NI), sds(NI, NS), sds(count, NS), sds(count, NE)),
        in_specs=[s, v, v, v, v],
        out_specs=(v,) * 6,
        scratch_shapes=[
            buf(TILE, NS), buf(TILE, 2 * NS), buf(TILE, 2 * NS),
            buf(64, 2 * NS), buf(64, 2 * NS), buf(64, 2 * NS), buf(64, 2 * NS),
            buf(16, 8, NS), buf(8, 8, 2 * NS), buf(8, 8, 2 * NS),
            buf(TILE, NS), buf(TILE, 2 * NS), buf(4, 8, 2 * NS), buf(4, 8, 2 * NS), buf(TILE, 2 * NS),
            buf(NE, NE), buf(3, TILE, TILE),
            dma((16,)), dma((2,)), dma((2, 8)), dma((3, 16)), dma((2, 4)), dma((82,)),
        ],
        compiler_params=pltpu.CompilerParams(collective_id=0, has_side_effects=True, vmem_limit_bytes=GRANT),
    )(tile_mask[0], ainv, coupling[0, 0], prior[0], sep_map)
    result, rows = pl.pallas_call(
        third_kernel,
        out_shape=(sds(NI, NI), sds(count, NRC)),
        in_specs=[v] * 8,
        out_specs=(v, v),
        scratch_shapes=[buf(NS, NS), buf(NS, NS)],
        compiler_params=pltpu.CompilerParams(vmem_limit_bytes=GRANT),
    )(total, nat_diag, sep_map, base, h, weights, b_rows, e_rows)
    return (result[None, None], rows[None])


def solution(mesh):
    placed = (
        P("region", "dev", None, None),
        P("region", "dev", None, None),
        P("region", "dev", None),
        P("region", "dev", None),
        P("region", None),
        P(),
    )
    return jax.shard_map(
        body,
        mesh=mesh,
        in_specs=placed,
        out_specs=(P("region", "dev", None, None), P("region", "dev", None)),
        check_vma=False,
    )
```

```python
import jax
import jax.numpy as jnp
from jax import lax
from jax.experimental import pallas as pl
from jax.experimental.pallas import tpu as pltpu
from jax.sharding import PartitionSpec as P

NI = 384
NE = 256
NS = 384
NRC = 640
TILE = 128
EXACT = lax.Precision.HIGHEST
F32 = jnp.float32
VMEM = pltpu.VMEM
GRANT = 24 * 1024 * 1024
MESH = pl.DeviceIdType.MESH


def dot(a, b, dims=((1,), (0,))):
    return lax.dot_general(a, b, (dims, ((), ())), precision=EXACT, preferred_element_type=F32)


def fast(a, b, dims=((1,), (0,))):
    return lax.dot_general(a, b, (dims, ((), ())), precision=lax.Precision.HIGH, preferred_element_type=F32)


def rough(a, b):
    return lax.dot_general(
        a.astype(jnp.bfloat16), b.astype(jnp.bfloat16), (((1,), (0,)), ((), ())), preferred_element_type=F32
    )


def split3(x):
    h = x.astype(jnp.bfloat16)
    rest = x - h.astype(F32)
    m = rest.astype(jnp.bfloat16)
    return h, m, (rest - m.astype(F32)).astype(jnp.bfloat16)


def select_right(x, onehot, dims=((1,), (0,))):
    h, m, l = (lax.dot_general(part, onehot, (dims, ((), ())), preferred_element_type=F32) for part in split3(x))
    return (h + m) + l


def select_left(onehot, x, dims=((1,), (0,))):
    h, m, l = (lax.dot_general(onehot, part, (dims, ((), ())), preferred_element_type=F32) for part in split3(x))
    return (h + m) + l


def row(x, k):
    return jnp.broadcast_to(x[k : k + 1, :], (8, 128))


def col(x, k):
    return jnp.broadcast_to(x[:, k : k + 1], (8, 128))


def recip(x):
    r = pl.reciprocal(x, approx=True)
    r = r * (2.0 - x * r)
    return r * (2.0 - x * r)


def inverse8(c, sub):
    c = list(c)
    for k in range(0, 8, 2):
        k1 = k + 1
        a, b, b2, e = row(c[k], k), row(c[k1], k), row(c[k], k1), row(c[k1], k1)
        rd = recip(a * e - b * b2)
        ia, ib, ib2, ie = e * rd, -(b * rd), -(b2 * rd), a * rd
        r0, r1 = sub == k, sub == k1
        ck, ck1 = c[k], c[k1]
        for j in range(8):
            if j in (k, k1):
                continue
            x, y = row(c[j], k), row(c[j], k1)
            m0, m1 = ia * x + ib * y, ib2 * x + ie * y
            c[j] = jnp.where(r0, m0, jnp.where(r1, m1, c[j] - (ck * m0 + ck1 * m1)))
        c[k] = jnp.where(r0, ia, jnp.where(r1, ib2, -(ck * ia + ck1 * ib2)))
        c[k1] = jnp.where(r0, ib, jnp.where(r1, ie, -(ck * ib + ck1 * ie)))
    return c


def sum8(t):
    return ((t[0] + t[1]) + (t[2] + t[3])) + ((t[4] + t[5]) + (t[6] + t[7]))


def inverse128(a):
    a = list(a)
    n = len(a)
    sub = lax.broadcasted_iota(jnp.int32, (8, 128), 0)
    lane = lax.broadcasted_iota(jnp.int32, (8, 128), 1)
    for p in range(n):
        lo = 8 * p
        r = a[p]
        d = inverse8([col(r, lo + j) for j in range(8)], sub)
        u = sum8([d[j] * row(r, j) for j in range(8)])
        for j in range(8):
            u = jnp.where(lane == lo + j, d[j], u)
        inside = (lane >= lo) & (lane < lo + 8)
        rows = [row(u, j) for j in range(8)]
        for step in range(n - 1):
            i = (p + 1 + step) % n
            x = a[i]
            a[i] = jnp.where(inside, 0.0, x) - sum8([col(x, lo + j) * rows[j] for j in range(8)])
        a[p] = u
    return a


def invert(w, blocks):
    def step(k, _):
        at = pl.ds(pl.multiple_of(k * TILE, TILE), TILE)
        full = w[at, at]
        pivot = jnp.concatenate(inverse128([full[8 * i : 8 * i + 8, :] for i in range(TILE // 8)]), axis=0)
        column = w[:, at]
        w[at, at] = jnp.zeros((TILE, TILE), F32)
        scaled = dot(pivot, w[at, :])
        w[:, at] = jnp.zeros((blocks * TILE, TILE), F32)
        w[...] = w[...] - dot(column, scaled)
        w[:, at] = -dot(column, pivot)
        w[at, :] = scaled
        w[at, at] = pivot
        return 0

    lax.fori_loop(0, blocks, step, 0)


def verified_inverse(a, x, low, steps):
    n = a.shape[0]
    eye = jnp.where(
        lax.broadcasted_iota(jnp.int32, (n, n), 0) == lax.broadcasted_iota(jnp.int32, (n, n), 1), 1.0, 0.0
    )
    full = a[...]
    high = jnp.max(jnp.sum(jnp.abs(full), axis=0, keepdims=True), axis=1, keepdims=True)
    c = 2.0 / (low + high)
    rho = (high - low) / (low + high)
    scale = 2.0 / (2.0 - rho * rho)
    x[...] = (2.0 * c * scale) * eye - (c * c * scale) * full
    rho = rho * rho / (2.0 - rho * rho)
    for _ in range(steps):
        scale = 2.0 / (2.0 - rho * rho)
        now = x[...]
        x[...] = (now * 2.0 - rough(now, rough(full, now))) * scale
        rho = rho * rho / (2.0 - rho * rho)

    def more(state):
        count, size = state
        return jnp.logical_and(count < 12, jnp.logical_not(size <= 1e-3))

    def step(state):
        count, _ = state
        now = x[...]
        r = eye - fast(a[...], now)
        x[...] = now + rough(now, r)
        return count + 1, jnp.sum(r * r)

    lax.while_loop(more, step, (jnp.int32(0), jnp.float32(1.0)))
    now = x[...]
    r = eye - dot(a[...], now)
    x[...] = now + rough(now, r)

    @pl.when(jnp.logical_not(jnp.sum(r * r) <= 1e-6))
    def _():
        x[...] = a[...]
        invert(x, n // TILE)


def national(sep_row):
    return (lax.broadcasted_iota(jnp.int32, (NS, NS), 0) == sep_row).astype(jnp.bfloat16)


def first_kernel(interior, ainv):
    verified_inverse(interior, ainv, 0.5, 4)


def second_kernel(
    mask, ainv, coupling, prior, sep, total, weights, base, h, b_rows, e_rows,
    e_own, x_own, s_own, half_x, half_s, acc_x, acc_s, rs_e, rs_x, rs_s, e_all, x_all, y_all, z_all, n_all,
    einv, tiles, e_sem, half_sem, rs_sem, ag_sem, reg_sem, send_sem,
):
    me, region = lax.axis_index("dev"), lax.axis_index("region")
    q, core = lax.div(me, 2), lax.rem(me, 2)
    y, z = lax.div(region, 4), lax.rem(region, 4)
    sent = []

    def send(src, dst, recv, **where):
        copy = pltpu.make_async_remote_copy(
            src_ref=src, dst_ref=dst, send_sem=send_sem.at[len(sent)], recv_sem=recv,
            device_id=where, device_id_type=MESH,
        )
        copy.start()
        sent.append(copy)

    def arrived(dst, recv):
        pltpu.make_async_remote_copy(
            src_ref=dst, dst_ref=dst, send_sem=send_sem.at[0], recv_sem=recv,
            device_id={"dev": lax.rem(me + 1, 16)}, device_id_type=MESH,
        ).wait_recv()

    others = [lax.rem(me + t, 16) for t in range(1, 16)]
    same_core = [lax.rem(q + t, 8) for t in range(1, 8)]
    y_peers = [lax.rem(y + t, 4) for t in range(1, 4)]
    z_peers = [lax.rem(z + t, 4) for t in range(1, 4)]

    barrier = pltpu.get_barrier_semaphore()
    for other in others:
        pl.semaphore_signal(barrier, inc=1, device_id={"dev": other}, device_id_type=MESH)
    for other in y_peers:
        pl.semaphore_signal(barrier, inc=1, device_id={"region": other * 4 + z}, device_id_type=MESH)
    for other in z_peers:
        pl.semaphore_signal(barrier, inc=1, device_id={"region": y * 4 + other}, device_id_type=MESH)

    partner = q * 2 + (1 - core)
    away = pl.ds(pl.multiple_of((1 - core) * 64, 64), 64)
    home = pl.ds(pl.multiple_of(core * 64, 64), 64)

    def rows_of(dev):
        return pl.ds(pl.multiple_of(lax.rem(dev, 2) * 64 + lax.div(dev, 2) * 8, 8), 8)

    def halve(kind, mine, half):
        send(mine.at[away, :], half.at[:, :], half_sem.at[kind], dev=partner)

    def scatter(kind, mine, half, acc, slots):
        arrived(half, half_sem.at[kind])
        acc[...] = mine[home, :] + half[...]
        for other in same_core:
            rows = pl.ds(pl.multiple_of(other * 8, 8), 8)
            send(acc.at[rows, :], slots.at[q], rs_sem.at[kind, q], dev=other * 2 + core)

    def gathered(kind, acc, slots):
        value = acc[pl.ds(pl.multiple_of(q * 8, 8), 8), :]
        for other in same_core:
            arrived(slots.at[other], rs_sem.at[kind, other])
            value = value + slots[other]
        return value

    def spread(kind, full):
        for other in others:
            send(full.at[rows_of(me), :], full.at[rows_of(me), :], ag_sem.at[kind, me], dev=other)

    def complete(kind, full):
        for other in others:
            arrived(full.at[rows_of(other), :], ag_sem.at[kind, other])

    count = prior.shape[0]
    perm = national(sep[...])
    m_e = jnp.concatenate([coupling[:, TILE * t : TILE * (t + 1)] * mask[0, t].astype(F32) for t in range(2)], axis=1)
    g_e = fast(ainv[...], m_e)
    at = lax.broadcasted_iota(jnp.int32, (NE, count), 1) + me * count
    place_e = (lax.broadcasted_iota(jnp.int32, (NE, count), 0) == at).astype(jnp.bfloat16)
    p_e = select_left(place_e, prior[:, :NE])
    e_own[:, :TILE] = p_e[:TILE, :TILE] - dot(m_e[:, :TILE], g_e[:, :TILE], ((0,), (0,)))
    e_own[:, TILE:] = p_e[TILE:, :] - dot(m_e[:, TILE:], g_e, ((0,), (0,)))
    pl.semaphore_wait(barrier, 21)
    for other in others:
        send(e_own.at[rows_of(other), :], rs_e.at[me], e_sem.at[me], dev=other)

    m_s = jnp.concatenate([coupling[:, TILE * t : TILE * (t + 1)] * mask[0, t].astype(F32) for t in range(2, 5)], axis=1)
    m_s = select_right(m_s, perm, ((1,), (1,)))
    g_s = fast(ainv[...], m_s)
    p_s = select_right(prior[:, NE:], perm, ((1,), (1,)))
    p_x = select_left(place_e, p_s)
    x_term = dot(m_e, g_s, ((0,), (0,)))
    x_own[:, :NS] = p_x[:TILE] - x_term[:TILE]
    x_own[:, NS:] = p_x[TILE:] - x_term[TILE:]
    halve(0, x_own, half_x)
    value = e_own[rows_of(me), :]
    for other in others:
        arrived(rs_e.at[other], e_sem.at[other])
        value = value + rs_e[other]
    e_all[rows_of(me), :] = value
    spread(0, e_all)
    scatter(0, x_own, half_x, acc_x, rs_x)
    at = lax.broadcasted_iota(jnp.int32, (NS, count), 1) + (me * count - NE)
    local = (lax.broadcasted_iota(jnp.int32, (NS, count), 0) == at).astype(jnp.bfloat16)
    place_s = lax.dot_general(perm, local, (((1,), (0,)), ((), ())), preferred_element_type=F32).astype(jnp.bfloat16)
    p_s = select_left(place_s, p_s)
    s_own[:, :TILE] = p_s[:TILE, :TILE] - dot(m_s[:, :TILE], g_s[:, :TILE], ((0,), (0,)))
    s_own[:, TILE : 3 * TILE] = p_s[TILE:NE, :NE] - dot(m_s[:, TILE:NE], g_s[:, :NE], ((0,), (0,)))
    s_own[:, 3 * TILE :] = p_s[NE:, :] - dot(m_s[:, NE:], g_s, ((0,), (0,)))
    halve(1, s_own, half_s)

    x_all[rows_of(me), :] = gathered(0, acc_x, rs_x)
    spread(1, x_all)
    scatter(1, s_own, half_s, acc_s, rs_s)

    complete(0, e_all)
    tiles[0] = e_all[:, :TILE]

    def pivot(k, _):
        block = tiles[k]
        tiles[k] = jnp.concatenate(inverse128([block[8 * i : 8 * i + 8, :] for i in range(TILE // 8)]), axis=0)

        @pl.when(k == 0)
        def _():
            tiles[2] = dot(e_all[:, TILE:NE], tiles[0])
            tiles[1] = e_all[:, NE:] - dot(tiles[2], e_all[:, TILE:NE], ((1,), (1,)))

        return 0

    lax.fori_loop(0, 2, pivot, 0)
    lower = dot(tiles[1], tiles[2])
    einv[:TILE, :TILE] = tiles[0] + dot(tiles[2], lower, ((0,), (0,)))
    einv[TILE:, :TILE] = -lower
    einv[:TILE, TILE:] = -lower.T
    einv[TILE:, TILE:] = tiles[1]
    complete(1, x_all)
    cross = jnp.concatenate([x_all[:, :NS], x_all[:, NS:]], axis=0)
    i0, i1 = (lax.broadcasted_iota(jnp.int32, (24, NS), d) for d in (0, 1))
    pick = (i1 == lax.div(i0, 8) * TILE + lax.rem(i0, 8) + core * 64 + q * 8).astype(jnp.bfloat16)
    part = dot(dot(select_left(pick, cross, ((1,), (1,))), einv[...]), cross)
    part = jnp.concatenate([part[:8, :TILE], part[8:16, :NE], part[16:, :]], axis=1)

    y_all[y] = gathered(1, acc_s, rs_s) - part
    for other in y_peers:
        send(y_all.at[y], y_all.at[y], reg_sem.at[0, y], region=other * 4 + z)
    w = dot(einv[...], cross)
    weights[...] = w
    h[...] = g_s - dot(g_e, w)
    for other in y_peers:
        arrived(y_all.at[other], reg_sem.at[0, other])
    z_all[z] = (y_all[0] + y_all[1]) + (y_all[2] + y_all[3])
    for other in z_peers:
        send(z_all.at[z], z_all.at[z], reg_sem.at[1, z], region=y * 4 + other)
    base[...] = ainv[...] + fast(dot(g_e, einv[...]), g_e, ((1,), (1,)))
    for other in z_peers:
        arrived(z_all.at[other], reg_sem.at[1, other])
    n_all[rows_of(me), :] = (z_all[0] + z_all[1]) + (z_all[2] + z_all[3])
    spread(2, n_all)
    at = lambda n: lax.broadcasted_iota(jnp.int32, (count, n), 0) + me * count
    pick_e = (lax.broadcasted_iota(jnp.int32, (count, NE), 1) == at(NE)).astype(jnp.bfloat16)
    pick_s = (lax.broadcasted_iota(jnp.int32, (count, NS), 1) + NE == at(NS)).astype(jnp.bfloat16)
    pick_s = lax.dot_general(pick_s, perm, (((1,), (1,)), ((), ())), preferred_element_type=F32)
    b_rows[...] = pick_s - select_left(pick_e, w)
    e_rows[...] = select_left(pick_e, einv[...])
    complete(2, n_all)
    total[...] = n_all[...]
    for copy in sent:
        copy.wait_send()


def third_kernel(total, diag, sep, base, h, weights, b_rows, e_rows, out, rows, normal, inverse):
    t0, t1, t2 = total[:, :TILE], total[:, TILE : 3 * TILE], total[:, 3 * TILE :]
    normal[:TILE, :TILE] = t0
    normal[TILE:NE, :NE] = t1
    normal[NE:, :] = t2
    normal[:TILE, TILE:NE] = t1[:, :TILE].T
    normal[:TILE, NE:] = t2[:, :TILE].T
    normal[TILE:NE, NE:] = t2[:, TILE:NE].T
    i0, i1 = (lax.broadcasted_iota(jnp.int32, (NS, NS), d) for d in (0, 1))
    normal[...] = normal[...] + jnp.where(i0 == i1, diag[...].reshape(1, NS), 0.0)
    verified_inverse(normal, inverse, 0.25, 3)
    x = inverse[...]
    w = weights[...]
    out[...] = base[...] + fast(fast(h[...], x), h[...], ((1,), (1,)))
    t = fast(b_rows[...], x)
    rows[:, :NE] = e_rows[...] - fast(t, w, ((1,), (1,)))
    rows[:, NE:] = select_right(t, national(sep[...]))


def body(interior, coupling, tile_mask, prior, sep_map, nat_diag):
    count = prior.shape[1]
    sds = lambda *shape: jax.ShapeDtypeStruct(shape, F32)
    v = pl.BlockSpec(memory_space=VMEM)
    s = pl.BlockSpec(memory_space=pltpu.SMEM)
    dma = pltpu.SemaphoreType.DMA
    buf = lambda *shape: VMEM(shape, F32)
    ainv = pl.pallas_call(
        first_kernel,
        out_shape=sds(NI, NI),
        in_specs=[v],
        out_specs=v,
        compiler_params=pltpu.CompilerParams(vmem_limit_bytes=GRANT),
    )(interior[0, 0])
    total, weights, base, h, b_rows, e_rows = pl.pallas_call(
        second_kernel,
        out_shape=(sds(TILE, 2 * NS), sds(NE, NS), sds(NI, NI), sds(NI, NS), sds(count, NS), sds(count, NE)),
        in_specs=[s, v, v, v, v],
        out_specs=(v,) * 6,
        scratch_shapes=[
            buf(TILE, NS), buf(TILE, 2 * NS), buf(TILE, 2 * NS),
            buf(64, 2 * NS), buf(64, 2 * NS), buf(64, 2 * NS), buf(64, 2 * NS),
            buf(16, 8, NS), buf(8, 8, 2 * NS), buf(8, 8, 2 * NS),
            buf(TILE, NS), buf(TILE, 2 * NS), buf(4, 8, 2 * NS), buf(4, 8, 2 * NS), buf(TILE, 2 * NS),
            buf(NE, NE), buf(3, TILE, TILE),
            dma((16,)), dma((2,)), dma((2, 8)), dma((3, 16)), dma((2, 4)), dma((82,)),
        ],
        compiler_params=pltpu.CompilerParams(collective_id=0, has_side_effects=True, vmem_limit_bytes=GRANT),
    )(tile_mask[0], ainv, coupling[0, 0], prior[0], sep_map)
    result, rows = pl.pallas_call(
        third_kernel,
        out_shape=(sds(NI, NI), sds(count, NRC)),
        in_specs=[v] * 8,
        out_specs=(v, v),
        scratch_shapes=[buf(NS, NS), buf(NS, NS)],
        compiler_params=pltpu.CompilerParams(vmem_limit_bytes=GRANT),
    )(total, nat_diag, sep_map, base, h, weights, b_rows, e_rows)
    return (result[None, None], rows[None])


def solution(mesh):
    placed = (
        P("region", "dev", None, None),
        P("region", "dev", None, None),
        P("region", "dev", None),
        P("region", "dev", None),
        P("region", None),
        P(),
    )
    return jax.shard_map(
        body,
        mesh=mesh,
        in_specs=placed,
        out_specs=(P("region", "dev", None, None), P("region", "dev", None)),
        check_vma=False,
    )
```

```python
import jax
import jax.numpy as jnp
from jax import lax
from jax.experimental import pallas as pl
from jax.experimental.pallas import tpu as pltpu
from jax.sharding import PartitionSpec as P

NI = 384
NE = 256
NS = 384
NRC = 640
TILE = 128
EXACT = lax.Precision.HIGHEST
F32 = jnp.float32
VMEM = pltpu.VMEM
GRANT = 24 * 1024 * 1024
MESH = pl.DeviceIdType.MESH


def dot(a, b, dims=((1,), (0,))):
    return lax.dot_general(a, b, (dims, ((), ())), precision=EXACT, preferred_element_type=F32)


def fast(a, b, dims=((1,), (0,))):
    return lax.dot_general(a, b, (dims, ((), ())), precision=lax.Precision.HIGH, preferred_element_type=F32)


def rough(a, b):
    return lax.dot_general(
        a.astype(jnp.bfloat16), b.astype(jnp.bfloat16), (((1,), (0,)), ((), ())), preferred_element_type=F32
    )


def split3(x):
    h = x.astype(jnp.bfloat16)
    rest = x - h.astype(F32)
    m = rest.astype(jnp.bfloat16)
    return h, m, (rest - m.astype(F32)).astype(jnp.bfloat16)


def select_right(x, onehot, dims=((1,), (0,))):
    h, m, l = (lax.dot_general(part, onehot, (dims, ((), ())), preferred_element_type=F32) for part in split3(x))
    return (h + m) + l


def select_left(onehot, x, dims=((1,), (0,))):
    h, m, l = (lax.dot_general(onehot, part, (dims, ((), ())), preferred_element_type=F32) for part in split3(x))
    return (h + m) + l


def row(x, k):
    return jnp.broadcast_to(x[k : k + 1, :], (8, 128))


def col(x, k):
    return jnp.broadcast_to(x[:, k : k + 1], (8, 128))


def recip(x):
    r = pl.reciprocal(x, approx=True)
    r = r * (2.0 - x * r)
    return r * (2.0 - x * r)


def inverse8(c, sub):
    c = list(c)
    for k in range(0, 8, 2):
        k1 = k + 1
        a, b, b2, e = row(c[k], k), row(c[k1], k), row(c[k], k1), row(c[k1], k1)
        rd = recip(a * e - b * b2)
        ia, ib, ib2, ie = e * rd, -(b * rd), -(b2 * rd), a * rd
        r0, r1 = sub == k, sub == k1
        ck, ck1 = c[k], c[k1]
        for j in range(8):
            if j in (k, k1):
                continue
            x, y = row(c[j], k), row(c[j], k1)
            m0, m1 = ia * x + ib * y, ib2 * x + ie * y
            c[j] = jnp.where(r0, m0, jnp.where(r1, m1, c[j] - (ck * m0 + ck1 * m1)))
        c[k] = jnp.where(r0, ia, jnp.where(r1, ib2, -(ck * ia + ck1 * ib2)))
        c[k1] = jnp.where(r0, ib, jnp.where(r1, ie, -(ck * ib + ck1 * ie)))
    return c


def sum8(t):
    return ((t[0] + t[1]) + (t[2] + t[3])) + ((t[4] + t[5]) + (t[6] + t[7]))


def inverse128(a):
    a = list(a)
    n = len(a)
    sub = lax.broadcasted_iota(jnp.int32, (8, 128), 0)
    lane = lax.broadcasted_iota(jnp.int32, (8, 128), 1)
    for p in range(n):
        lo = 8 * p
        r = a[p]
        d = inverse8([col(r, lo + j) for j in range(8)], sub)
        u = sum8([d[j] * row(r, j) for j in range(8)])
        for j in range(8):
            u = jnp.where(lane == lo + j, d[j], u)
        inside = (lane >= lo) & (lane < lo + 8)
        rows = [row(u, j) for j in range(8)]
        for step in range(n - 1):
            i = (p + 1 + step) % n
            x = a[i]
            a[i] = jnp.where(inside, 0.0, x) - sum8([col(x, lo + j) * rows[j] for j in range(8)])
        a[p] = u
    return a


def invert(w, blocks):
    def step(k, _):
        at = pl.ds(pl.multiple_of(k * TILE, TILE), TILE)
        full = w[at, at]
        pivot = jnp.concatenate(inverse128([full[8 * i : 8 * i + 8, :] for i in range(TILE // 8)]), axis=0)
        column = w[:, at]
        w[at, at] = jnp.zeros((TILE, TILE), F32)
        scaled = dot(pivot, w[at, :])
        w[:, at] = jnp.zeros((blocks * TILE, TILE), F32)
        w[...] = w[...] - dot(column, scaled)
        w[:, at] = -dot(column, pivot)
        w[at, :] = scaled
        w[at, at] = pivot
        return 0

    lax.fori_loop(0, blocks, step, 0)


def verified_inverse(a, x, low, steps):
    n = a.shape[0]
    eye = jnp.where(
        lax.broadcasted_iota(jnp.int32, (n, n), 0) == lax.broadcasted_iota(jnp.int32, (n, n), 1), 1.0, 0.0
    )
    full = a[...]
    high = jnp.max(jnp.sum(jnp.abs(full), axis=0, keepdims=True), axis=1, keepdims=True)
    c = 2.0 / (low + high)
    rho = (high - low) / (low + high)
    scale = 2.0 / (2.0 - rho * rho)
    x[...] = (2.0 * c * scale) * eye - (c * c * scale) * full
    rho = rho * rho / (2.0 - rho * rho)
    for _ in range(steps):
        scale = 2.0 / (2.0 - rho * rho)
        now = x[...]
        x[...] = (now * 2.0 - rough(now, rough(full, now))) * scale
        rho = rho * rho / (2.0 - rho * rho)

    def more(state):
        count, size = state
        return jnp.logical_and(count < 12, jnp.logical_not(size <= 1e-3))

    def step(state):
        count, _ = state
        now = x[...]
        r = eye - fast(a[...], now)
        x[...] = now + rough(now, r)
        return count + 1, jnp.sum(r * r)

    lax.while_loop(more, step, (jnp.int32(0), jnp.float32(1.0)))
    now = x[...]
    r = eye - dot(a[...], now)
    x[...] = now + rough(now, r)

    @pl.when(jnp.logical_not(jnp.sum(r * r) <= 1e-6))
    def _():
        x[...] = a[...]
        invert(x, n // TILE)


def national(sep_row):
    return (lax.broadcasted_iota(jnp.int32, (NS, NS), 0) == sep_row).astype(jnp.bfloat16)


def first_kernel(interior, ainv):
    verified_inverse(interior, ainv, 0.5, 4)


def second_kernel(
    mask, ainv, coupling, prior, sep, diag, normal, weights, base, h, b_rows, e_rows,
    e_own, x_own, s_own, half_x, half_s, acc_x, acc_s, rs_e, rs_x, rs_s, e_all, x_all, y_all, z_all, n_all,
    einv, tiles, e_sem, half_sem, rs_sem, ag_sem, reg_sem, send_sem,
):
    me, region = lax.axis_index("dev"), lax.axis_index("region")
    q, core = lax.div(me, 2), lax.rem(me, 2)
    y, z = lax.div(region, 4), lax.rem(region, 4)
    sent = []

    def send(src, dst, recv, **where):
        copy = pltpu.make_async_remote_copy(
            src_ref=src, dst_ref=dst, send_sem=send_sem.at[len(sent)], recv_sem=recv,
            device_id=where, device_id_type=MESH,
        )
        copy.start()
        sent.append(copy)

    def arrived(dst, recv):
        pltpu.make_async_remote_copy(
            src_ref=dst, dst_ref=dst, send_sem=send_sem.at[0], recv_sem=recv,
            device_id={"dev": lax.rem(me + 1, 16)}, device_id_type=MESH,
        ).wait_recv()

    others = [lax.rem(me + t, 16) for t in range(1, 16)]
    same_core = [lax.rem(q + t, 8) for t in range(1, 8)]
    y_peers = [lax.rem(y + t, 4) for t in range(1, 4)]
    z_peers = [lax.rem(z + t, 4) for t in range(1, 4)]

    barrier = pltpu.get_barrier_semaphore()
    for other in others:
        pl.semaphore_signal(barrier, inc=1, device_id={"dev": other}, device_id_type=MESH)
    for other in y_peers:
        pl.semaphore_signal(barrier, inc=1, device_id={"region": other * 4 + z}, device_id_type=MESH)
    for other in z_peers:
        pl.semaphore_signal(barrier, inc=1, device_id={"region": y * 4 + other}, device_id_type=MESH)

    partner = q * 2 + (1 - core)
    away = pl.ds(pl.multiple_of((1 - core) * 64, 64), 64)
    home = pl.ds(pl.multiple_of(core * 64, 64), 64)

    def rows_of(dev):
        return pl.ds(pl.multiple_of(lax.rem(dev, 2) * 64 + lax.div(dev, 2) * 8, 8), 8)

    def halve(kind, mine, half):
        send(mine.at[away, :], half.at[:, :], half_sem.at[kind], dev=partner)

    def scatter(kind, mine, half, acc, slots):
        arrived(half, half_sem.at[kind])
        acc[...] = mine[home, :] + half[...]
        for other in same_core:
            rows = pl.ds(pl.multiple_of(other * 8, 8), 8)
            send(acc.at[rows, :], slots.at[q], rs_sem.at[kind, q], dev=other * 2 + core)

    def gathered(kind, acc, slots):
        value = acc[pl.ds(pl.multiple_of(q * 8, 8), 8), :]
        for other in same_core:
            arrived(slots.at[other], rs_sem.at[kind, other])
            value = value + slots[other]
        return value

    def spread(kind, full):
        for other in others:
            send(full.at[rows_of(me), :], full.at[rows_of(me), :], ag_sem.at[kind, me], dev=other)

    def complete(kind, full):
        for other in others:
            arrived(full.at[rows_of(other), :], ag_sem.at[kind, other])

    def near(kind, full):
        for dev in [other * 2 + core for other in same_core] + [partner]:
            send(full.at[rows_of(me), :], full.at[rows_of(me), :], ag_sem.at[kind, me], dev=dev)

    def far(kind, full):
        for other in same_core:
            dev = other * 2 + core
            arrived(full.at[rows_of(dev), :], ag_sem.at[kind, dev])
            send(full.at[rows_of(dev), :], full.at[rows_of(dev), :], ag_sem.at[kind, dev], dev=partner)
        for dev in [partner] + [other * 2 + 1 - core for other in same_core]:
            arrived(full.at[rows_of(dev), :], ag_sem.at[kind, dev])

    count = prior.shape[0]
    perm = national(sep[...])
    m_e = jnp.concatenate([coupling[:, TILE * t : TILE * (t + 1)] * mask[0, t].astype(F32) for t in range(2)], axis=1)
    g_e = fast(ainv[...], m_e)
    at = lax.broadcasted_iota(jnp.int32, (NE, count), 1) + me * count
    place_e = (lax.broadcasted_iota(jnp.int32, (NE, count), 0) == at).astype(jnp.bfloat16)
    p_e = select_left(place_e, prior[:, :NE])
    e_own[:, :TILE] = p_e[:TILE, :TILE] - dot(m_e[:, :TILE], g_e[:, :TILE], ((0,), (0,)))
    e_own[:, TILE:] = p_e[TILE:, :] - dot(m_e[:, TILE:], g_e, ((0,), (0,)))
    pl.semaphore_wait(barrier, 21)
    for other in others:
        send(e_own.at[rows_of(other), :], rs_e.at[me], e_sem.at[me], dev=other)

    m_s = jnp.concatenate([coupling[:, TILE * t : TILE * (t + 1)] * mask[0, t].astype(F32) for t in range(2, 5)], axis=1)
    m_s = select_right(m_s, perm, ((1,), (1,)))
    g_s = fast(ainv[...], m_s)
    p_s = select_right(prior[:, NE:], perm, ((1,), (1,)))
    p_x = select_left(place_e, p_s)
    x_term = dot(m_e, g_s, ((0,), (0,)))
    x_own[:, :NS] = p_x[:TILE] - x_term[:TILE]
    x_own[:, NS:] = p_x[TILE:] - x_term[TILE:]
    halve(0, x_own, half_x)
    value = e_own[rows_of(me), :]
    for other in others:
        arrived(rs_e.at[other], e_sem.at[other])
        value = value + rs_e[other]
    e_all[rows_of(me), :] = value
    spread(0, e_all)
    scatter(0, x_own, half_x, acc_x, rs_x)
    at = lax.broadcasted_iota(jnp.int32, (NS, count), 1) + (me * count - NE)
    local = (lax.broadcasted_iota(jnp.int32, (NS, count), 0) == at).astype(jnp.bfloat16)
    place_s = lax.dot_general(perm, local, (((1,), (0,)), ((), ())), preferred_element_type=F32).astype(jnp.bfloat16)
    p_s = select_left(place_s, p_s)
    s_own[:, :TILE] = p_s[:TILE, :TILE] - dot(m_s[:, :TILE], g_s[:, :TILE], ((0,), (0,)))
    s_own[:, TILE : 3 * TILE] = p_s[TILE:NE, :NE] - dot(m_s[:, TILE:NE], g_s[:, :NE], ((0,), (0,)))
    s_own[:, 3 * TILE :] = p_s[NE:, :] - dot(m_s[:, NE:], g_s, ((0,), (0,)))
    halve(1, s_own, half_s)

    x_all[rows_of(me), :] = gathered(0, acc_x, rs_x)
    spread(1, x_all)
    scatter(1, s_own, half_s, acc_s, rs_s)

    complete(0, e_all)
    tiles[0] = e_all[:, :TILE]

    def pivot(k, _):
        block = tiles[k]
        tiles[k] = jnp.concatenate(inverse128([block[8 * i : 8 * i + 8, :] for i in range(TILE // 8)]), axis=0)

        @pl.when(k == 0)
        def _():
            tiles[2] = dot(e_all[:, TILE:NE], tiles[0])
            tiles[1] = e_all[:, NE:] - dot(tiles[2], e_all[:, TILE:NE], ((1,), (1,)))

        return 0

    lax.fori_loop(0, 2, pivot, 0)
    lower = dot(tiles[1], tiles[2])
    einv[:TILE, :TILE] = tiles[0] + dot(tiles[2], lower, ((0,), (0,)))
    einv[TILE:, :TILE] = -lower
    einv[:TILE, TILE:] = -lower.T
    einv[TILE:, TILE:] = tiles[1]
    complete(1, x_all)
    cross = jnp.concatenate([x_all[:, :NS], x_all[:, NS:]], axis=0)
    i0, i1 = (lax.broadcasted_iota(jnp.int32, (24, NS), d) for d in (0, 1))
    pick = (i1 == lax.div(i0, 8) * TILE + lax.rem(i0, 8) + core * 64 + q * 8).astype(jnp.bfloat16)
    part = dot(dot(select_left(pick, cross, ((1,), (1,))), einv[...]), cross)
    part = jnp.concatenate([part[:8, :TILE], part[8:16, :NE], part[16:, :]], axis=1)

    y_all[y] = gathered(1, acc_s, rs_s) - part
    for other in y_peers:
        send(y_all.at[y], y_all.at[y], reg_sem.at[0, y], region=other * 4 + z)
    w = dot(einv[...], cross)
    weights[...] = w
    h[...] = g_s - dot(g_e, w)
    for other in y_peers:
        arrived(y_all.at[other], reg_sem.at[0, other])
    z_all[z] = (y_all[0] + y_all[1]) + (y_all[2] + y_all[3])
    for other in z_peers:
        send(z_all.at[z], z_all.at[z], reg_sem.at[1, z], region=y * 4 + other)
    base[...] = ainv[...] + fast(dot(g_e, einv[...]), g_e, ((1,), (1,)))
    for other in z_peers:
        arrived(z_all.at[other], reg_sem.at[1, other])
    n_all[rows_of(me), :] = (z_all[0] + z_all[1]) + (z_all[2] + z_all[3])
    near(2, n_all)
    at = lambda n: lax.broadcasted_iota(jnp.int32, (count, n), 0) + me * count
    pick_e = (lax.broadcasted_iota(jnp.int32, (count, NE), 1) == at(NE)).astype(jnp.bfloat16)
    pick_s = (lax.broadcasted_iota(jnp.int32, (count, NS), 1) + NE == at(NS)).astype(jnp.bfloat16)
    pick_s = lax.dot_general(pick_s, perm, (((1,), (1,)), ((), ())), preferred_element_type=F32)
    b_rows[...] = pick_s - select_left(pick_e, w)
    e_rows[...] = select_left(pick_e, einv[...])
    far(2, n_all)
    i0, i1 = (lax.broadcasted_iota(jnp.int32, (NS, NS), d) for d in (0, 1))
    t0, t1, t2 = n_all[:, :TILE], n_all[:, TILE : 3 * TILE], n_all[:, 3 * TILE :]
    normal[:TILE, :TILE] = t0
    normal[TILE:NE, :NE] = t1
    normal[NE:, :] = t2
    normal[:TILE, TILE:NE] = t1[:, :TILE].T
    normal[:TILE, NE:] = t2[:, :TILE].T
    normal[TILE:NE, NE:] = t2[:, TILE:NE].T
    normal[...] = normal[...] + jnp.where(i0 == i1, diag[...].reshape(1, NS), 0.0)
    for copy in sent:
        copy.wait_send()


def third_kernel(normal, sep, base, h, weights, b_rows, e_rows, out, rows, inverse):
    verified_inverse(normal, inverse, 0.25, 3)
    x = inverse[...]
    w = weights[...]
    out[...] = base[...] + fast(fast(h[...], x), h[...], ((1,), (1,)))
    t = fast(b_rows[...], x)
    rows[:, :NE] = e_rows[...] - fast(t, w, ((1,), (1,)))
    rows[:, NE:] = select_right(t, national(sep[...]))


def body(interior, coupling, tile_mask, prior, sep_map, nat_diag):
    count = prior.shape[1]
    sds = lambda *shape: jax.ShapeDtypeStruct(shape, F32)
    v = pl.BlockSpec(memory_space=VMEM)
    s = pl.BlockSpec(memory_space=pltpu.SMEM)
    dma = pltpu.SemaphoreType.DMA
    buf = lambda *shape: VMEM(shape, F32)
    ainv = pl.pallas_call(
        first_kernel,
        out_shape=sds(NI, NI),
        in_specs=[v],
        out_specs=v,
        compiler_params=pltpu.CompilerParams(vmem_limit_bytes=GRANT),
    )(interior[0, 0])
    normal, weights, base, h, b_rows, e_rows = pl.pallas_call(
        second_kernel,
        out_shape=(sds(NS, NS), sds(NE, NS), sds(NI, NI), sds(NI, NS), sds(count, NS), sds(count, NE)),
        in_specs=[s, v, v, v, v, v],
        out_specs=(v,) * 6,
        scratch_shapes=[
            buf(TILE, NS), buf(TILE, 2 * NS), buf(TILE, 2 * NS),
            buf(64, 2 * NS), buf(64, 2 * NS), buf(64, 2 * NS), buf(64, 2 * NS),
            buf(16, 8, NS), buf(8, 8, 2 * NS), buf(8, 8, 2 * NS),
            buf(TILE, NS), buf(TILE, 2 * NS), buf(4, 8, 2 * NS), buf(4, 8, 2 * NS), buf(TILE, 2 * NS),
            buf(NE, NE), buf(3, TILE, TILE),
            dma((16,)), dma((2,)), dma((2, 8)), dma((3, 16)), dma((2, 4)), dma((82,)),
        ],
        compiler_params=pltpu.CompilerParams(collective_id=0, has_side_effects=True, vmem_limit_bytes=GRANT),
    )(tile_mask[0], ainv, coupling[0, 0], prior[0], sep_map, nat_diag)
    result, rows = pl.pallas_call(
        third_kernel,
        out_shape=(sds(NI, NI), sds(count, NRC)),
        in_specs=[v] * 7,
        out_specs=(v, v),
        scratch_shapes=[buf(NS, NS)],
        compiler_params=pltpu.CompilerParams(vmem_limit_bytes=GRANT),
    )(normal, sep_map, base, h, weights, b_rows, e_rows)
    return (result[None, None], rows[None])


def solution(mesh):
    placed = (
        P("region", "dev", None, None),
        P("region", "dev", None, None),
        P("region", "dev", None),
        P("region", "dev", None),
        P("region", None),
        P(),
    )
    return jax.shard_map(
        body,
        mesh=mesh,
        in_specs=placed,
        out_specs=(P("region", "dev", None, None), P("region", "dev", None)),
        check_vma=False,
    )
```

```python
import jax
import jax.numpy as jnp
from jax import lax
from jax.experimental import pallas as pl
from jax.experimental.pallas import tpu as pltpu
from jax.sharding import PartitionSpec as P

NI = 384
NE = 256
NS = 384
NRC = 640
TILE = 128
EXACT = lax.Precision.HIGHEST
F32 = jnp.float32
VMEM = pltpu.VMEM
GRANT = 24 * 1024 * 1024
MESH = pl.DeviceIdType.MESH


def dot(a, b, dims=((1,), (0,))):
    return lax.dot_general(a, b, (dims, ((), ())), precision=EXACT, preferred_element_type=F32)


def fast(a, b, dims=((1,), (0,))):
    return lax.dot_general(a, b, (dims, ((), ())), precision=lax.Precision.HIGH, preferred_element_type=F32)


def rough(a, b):
    return lax.dot_general(
        a.astype(jnp.bfloat16), b.astype(jnp.bfloat16), (((1,), (0,)), ((), ())), preferred_element_type=F32
    )


def split3(x):
    h = x.astype(jnp.bfloat16)
    rest = x - h.astype(F32)
    m = rest.astype(jnp.bfloat16)
    return h, m, (rest - m.astype(F32)).astype(jnp.bfloat16)


def select_right(x, onehot, dims=((1,), (0,))):
    h, m, l = (lax.dot_general(part, onehot, (dims, ((), ())), preferred_element_type=F32) for part in split3(x))
    return (h + m) + l


def select_left(onehot, x, dims=((1,), (0,))):
    h, m, l = (lax.dot_general(onehot, part, (dims, ((), ())), preferred_element_type=F32) for part in split3(x))
    return (h + m) + l


def row(x, k):
    return jnp.broadcast_to(x[k : k + 1, :], (8, 128))


def col(x, k):
    return jnp.broadcast_to(x[:, k : k + 1], (8, 128))


def recip(x):
    r = pl.reciprocal(x, approx=True)
    r = r * (2.0 - x * r)
    return r * (2.0 - x * r)


def inverse8(c, sub):
    c = list(c)
    for k in range(0, 8, 2):
        k1 = k + 1
        a, b, b2, e = row(c[k], k), row(c[k1], k), row(c[k], k1), row(c[k1], k1)
        rd = recip(a * e - b * b2)
        ia, ib, ib2, ie = e * rd, -(b * rd), -(b2 * rd), a * rd
        r0, r1 = sub == k, sub == k1
        ck, ck1 = c[k], c[k1]
        for j in range(8):
            if j in (k, k1):
                continue
            x, y = row(c[j], k), row(c[j], k1)
            m0, m1 = ia * x + ib * y, ib2 * x + ie * y
            c[j] = jnp.where(r0, m0, jnp.where(r1, m1, c[j] - (ck * m0 + ck1 * m1)))
        c[k] = jnp.where(r0, ia, jnp.where(r1, ib2, -(ck * ia + ck1 * ib2)))
        c[k1] = jnp.where(r0, ib, jnp.where(r1, ie, -(ck * ib + ck1 * ie)))
    return c


def sum8(t):
    return ((t[0] + t[1]) + (t[2] + t[3])) + ((t[4] + t[5]) + (t[6] + t[7]))


def inverse128(a):
    a = list(a)
    n = len(a)
    sub = lax.broadcasted_iota(jnp.int32, (8, 128), 0)
    lane = lax.broadcasted_iota(jnp.int32, (8, 128), 1)
    for p in range(n):
        lo = 8 * p
        r = a[p]
        d = inverse8([col(r, lo + j) for j in range(8)], sub)
        u = sum8([d[j] * row(r, j) for j in range(8)])
        for j in range(8):
            u = jnp.where(lane == lo + j, d[j], u)
        inside = (lane >= lo) & (lane < lo + 8)
        rows = [row(u, j) for j in range(8)]
        for step in range(n - 1):
            i = (p + 1 + step) % n
            x = a[i]
            a[i] = jnp.where(inside, 0.0, x) - sum8([col(x, lo + j) * rows[j] for j in range(8)])
        a[p] = u
    return a


def invert(w, blocks):
    def step(k, _):
        at = pl.ds(pl.multiple_of(k * TILE, TILE), TILE)
        full = w[at, at]
        pivot = jnp.concatenate(inverse128([full[8 * i : 8 * i + 8, :] for i in range(TILE // 8)]), axis=0)
        column = w[:, at]
        w[at, at] = jnp.zeros((TILE, TILE), F32)
        scaled = dot(pivot, w[at, :])
        w[:, at] = jnp.zeros((blocks * TILE, TILE), F32)
        w[...] = w[...] - dot(column, scaled)
        w[:, at] = -dot(column, pivot)
        w[at, :] = scaled
        w[at, at] = pivot
        return 0

    lax.fori_loop(0, blocks, step, 0)


def verified_inverse(a, x, low, steps):
    n = a.shape[0]
    eye = jnp.where(
        lax.broadcasted_iota(jnp.int32, (n, n), 0) == lax.broadcasted_iota(jnp.int32, (n, n), 1), 1.0, 0.0
    )
    full = a[...]
    high = jnp.max(jnp.sum(jnp.abs(full), axis=0, keepdims=True), axis=1, keepdims=True)
    c = 2.0 / (low + high)
    rho = (high - low) / (low + high)
    scale = 2.0 / (2.0 - rho * rho)
    x[...] = (2.0 * c * scale) * eye - (c * c * scale) * full
    rho = rho * rho / (2.0 - rho * rho)
    for _ in range(steps):
        scale = 2.0 / (2.0 - rho * rho)
        now = x[...]
        x[...] = (now + rough(now, eye - rough(full, now))) * scale
        rho = rho * rho / (2.0 - rho * rho)

    def refine(multiply, limit, most):
        def more(state):
            count, size = state
            return jnp.logical_and(count < most, jnp.logical_not(size <= limit))

        def step(state):
            count, _ = state
            now = x[...]
            r = eye - multiply(a[...], now)
            x[...] = now + rough(now, r)
            return count + 1, jnp.sum(r * r)

        return lax.while_loop(more, step, (jnp.int32(0), jnp.float32(1.0)))[1]

    refine(fast, 1e-2, 12)
    size = refine(dot, 4e-6, 4)

    @pl.when(jnp.logical_not(size <= 4e-6))
    def _():
        x[...] = a[...]
        invert(x, n // TILE)


def national(sep_row):
    return (lax.broadcasted_iota(jnp.int32, (NS, NS), 0) == sep_row).astype(jnp.bfloat16)


def first_kernel(interior, ainv):
    verified_inverse(interior, ainv, 0.5, 4)


def second_kernel(
    mask, ainv, coupling, prior, sep, diag, normal, weights, base, h, b_rows, e_rows,
    e_own, x_own, s_own, half_x, half_s, acc_x, acc_s, rs_e, rs_x, rs_s, e_all, x_all, y_all, z_all, n_all,
    einv, tiles, e_sem, half_sem, rs_sem, ag_sem, reg_sem, send_sem,
):
    me, region = lax.axis_index("dev"), lax.axis_index("region")
    q, core = lax.div(me, 2), lax.rem(me, 2)
    y, z = lax.div(region, 4), lax.rem(region, 4)
    sent = []

    def send(src, dst, recv, **where):
        copy = pltpu.make_async_remote_copy(
            src_ref=src, dst_ref=dst, send_sem=send_sem.at[len(sent)], recv_sem=recv,
            device_id=where, device_id_type=MESH,
        )
        copy.start()
        sent.append(copy)

    def arrived(dst, recv):
        pltpu.make_async_remote_copy(
            src_ref=dst, dst_ref=dst, send_sem=send_sem.at[0], recv_sem=recv,
            device_id={"dev": lax.rem(me + 1, 16)}, device_id_type=MESH,
        ).wait_recv()

    others = [lax.rem(me + t, 16) for t in range(1, 16)]
    same_core = [lax.rem(q + t, 8) for t in range(1, 8)]
    y_peers = [lax.rem(y + t, 4) for t in range(1, 4)]
    z_peers = [lax.rem(z + t, 4) for t in range(1, 4)]

    barrier = pltpu.get_barrier_semaphore()
    for other in others:
        pl.semaphore_signal(barrier, inc=1, device_id={"dev": other}, device_id_type=MESH)
    for other in y_peers:
        pl.semaphore_signal(barrier, inc=1, device_id={"region": other * 4 + z}, device_id_type=MESH)
    for other in z_peers:
        pl.semaphore_signal(barrier, inc=1, device_id={"region": y * 4 + other}, device_id_type=MESH)

    partner = q * 2 + (1 - core)
    away = pl.ds(pl.multiple_of((1 - core) * 64, 64), 64)
    home = pl.ds(pl.multiple_of(core * 64, 64), 64)

    def rows_of(dev):
        return pl.ds(pl.multiple_of(lax.rem(dev, 2) * 64 + lax.div(dev, 2) * 8, 8), 8)

    def halve(kind, mine, half):
        send(mine.at[away, :], half.at[:, :], half_sem.at[kind], dev=partner)

    def scatter(kind, mine, half, acc, slots):
        arrived(half, half_sem.at[kind])
        acc[...] = mine[home, :] + half[...]
        for other in same_core:
            rows = pl.ds(pl.multiple_of(other * 8, 8), 8)
            send(acc.at[rows, :], slots.at[q], rs_sem.at[kind, q], dev=other * 2 + core)

    def gathered(kind, acc, slots):
        value = acc[pl.ds(pl.multiple_of(q * 8, 8), 8), :]
        for other in same_core:
            arrived(slots.at[other], rs_sem.at[kind, other])
            value = value + slots[other]
        return value

    def spread(kind, full):
        for other in others:
            send(full.at[rows_of(me), :], full.at[rows_of(me), :], ag_sem.at[kind, me], dev=other)

    def complete(kind, full):
        for other in others:
            arrived(full.at[rows_of(other), :], ag_sem.at[kind, other])

    def near(kind, full):
        for dev in [other * 2 + core for other in same_core] + [partner]:
            send(full.at[rows_of(me), :], full.at[rows_of(me), :], ag_sem.at[kind, me], dev=dev)

    def far(kind, full):
        for other in same_core:
            dev = other * 2 + core
            arrived(full.at[rows_of(dev), :], ag_sem.at[kind, dev])
            send(full.at[rows_of(dev), :], full.at[rows_of(dev), :], ag_sem.at[kind, dev], dev=partner)
        for dev in [partner] + [other * 2 + 1 - core for other in same_core]:
            arrived(full.at[rows_of(dev), :], ag_sem.at[kind, dev])

    count = prior.shape[0]
    perm = national(sep[...])
    m_e = jnp.concatenate([coupling[:, TILE * t : TILE * (t + 1)] * mask[0, t].astype(F32) for t in range(2)], axis=1)
    g_e = fast(ainv[...], m_e)
    at = lax.broadcasted_iota(jnp.int32, (NE, count), 1) + me * count
    place_e = (lax.broadcasted_iota(jnp.int32, (NE, count), 0) == at).astype(jnp.bfloat16)
    p_e = select_left(place_e, prior[:, :NE])
    e_own[:, :TILE] = p_e[:TILE, :TILE] - dot(m_e[:, :TILE], g_e[:, :TILE], ((0,), (0,)))
    e_own[:, TILE:] = p_e[TILE:, :] - dot(m_e[:, TILE:], g_e, ((0,), (0,)))
    pl.semaphore_wait(barrier, 21)
    for other in others:
        send(e_own.at[rows_of(other), :], rs_e.at[me], e_sem.at[me], dev=other)

    m_s = jnp.concatenate([coupling[:, TILE * t : TILE * (t + 1)] * mask[0, t].astype(F32) for t in range(2, 5)], axis=1)
    m_s = select_right(m_s, perm, ((1,), (1,)))
    g_s = fast(ainv[...], m_s)
    p_s = select_right(prior[:, NE:], perm, ((1,), (1,)))
    p_x = select_left(place_e, p_s)
    x_term = dot(m_e, g_s, ((0,), (0,)))
    x_own[:, :NS] = p_x[:TILE] - x_term[:TILE]
    x_own[:, NS:] = p_x[TILE:] - x_term[TILE:]
    halve(0, x_own, half_x)
    value = e_own[rows_of(me), :]
    for other in others:
        arrived(rs_e.at[other], e_sem.at[other])
        value = value + rs_e[other]
    e_all[rows_of(me), :] = value
    spread(0, e_all)
    scatter(0, x_own, half_x, acc_x, rs_x)
    at = lax.broadcasted_iota(jnp.int32, (NS, count), 1) + (me * count - NE)
    local = (lax.broadcasted_iota(jnp.int32, (NS, count), 0) == at).astype(jnp.bfloat16)
    place_s = lax.dot_general(perm, local, (((1,), (0,)), ((), ())), preferred_element_type=F32).astype(jnp.bfloat16)
    p_s = select_left(place_s, p_s)
    s_own[:, :TILE] = p_s[:TILE, :TILE] - dot(m_s[:, :TILE], g_s[:, :TILE], ((0,), (0,)))
    s_own[:, TILE : 3 * TILE] = p_s[TILE:NE, :NE] - dot(m_s[:, TILE:NE], g_s[:, :NE], ((0,), (0,)))
    s_own[:, 3 * TILE :] = p_s[NE:, :] - dot(m_s[:, NE:], g_s, ((0,), (0,)))
    halve(1, s_own, half_s)

    x_all[rows_of(me), :] = gathered(0, acc_x, rs_x)
    spread(1, x_all)
    scatter(1, s_own, half_s, acc_s, rs_s)

    complete(0, e_all)
    tiles[0] = e_all[:, :TILE]

    def pivot(k, _):
        block = tiles[k]
        tiles[k] = jnp.concatenate(inverse128([block[8 * i : 8 * i + 8, :] for i in range(TILE // 8)]), axis=0)

        @pl.when(k == 0)
        def _():
            tiles[2] = dot(e_all[:, TILE:NE], tiles[0])
            tiles[1] = e_all[:, NE:] - dot(tiles[2], e_all[:, TILE:NE], ((1,), (1,)))

        return 0

    lax.fori_loop(0, 2, pivot, 0)
    lower = dot(tiles[1], tiles[2])
    einv[:TILE, :TILE] = tiles[0] + dot(tiles[2], lower, ((0,), (0,)))
    einv[TILE:, :TILE] = -lower
    einv[:TILE, TILE:] = -lower.T
    einv[TILE:, TILE:] = tiles[1]
    complete(1, x_all)
    cross = jnp.concatenate([x_all[:, :NS], x_all[:, NS:]], axis=0)
    i0, i1 = (lax.broadcasted_iota(jnp.int32, (24, NS), d) for d in (0, 1))
    pick = (i1 == lax.div(i0, 8) * TILE + lax.rem(i0, 8) + core * 64 + q * 8).astype(jnp.bfloat16)
    part = dot(dot(select_left(pick, cross, ((1,), (1,))), einv[...]), cross)
    part = jnp.concatenate([part[:8, :TILE], part[8:16, :NE], part[16:, :]], axis=1)

    y_all[y] = gathered(1, acc_s, rs_s) - part
    for other in y_peers:
        send(y_all.at[y], y_all.at[y], reg_sem.at[0, y], region=other * 4 + z)
    w = dot(einv[...], cross)
    weights[...] = w
    h[...] = g_s - dot(g_e, w)
    for other in y_peers:
        arrived(y_all.at[other], reg_sem.at[0, other])
    z_all[z] = (y_all[0] + y_all[1]) + (y_all[2] + y_all[3])
    for other in z_peers:
        send(z_all.at[z], z_all.at[z], reg_sem.at[1, z], region=y * 4 + other)
    base[...] = ainv[...] + fast(dot(g_e, einv[...]), g_e, ((1,), (1,)))
    for other in z_peers:
        arrived(z_all.at[other], reg_sem.at[1, other])
    n_all[rows_of(me), :] = (z_all[0] + z_all[1]) + (z_all[2] + z_all[3])
    near(2, n_all)
    at = lambda n: lax.broadcasted_iota(jnp.int32, (count, n), 0) + me * count
    pick_e = (lax.broadcasted_iota(jnp.int32, (count, NE), 1) == at(NE)).astype(jnp.bfloat16)
    pick_s = (lax.broadcasted_iota(jnp.int32, (count, NS), 1) + NE == at(NS)).astype(jnp.bfloat16)
    pick_s = lax.dot_general(pick_s, perm, (((1,), (1,)), ((), ())), preferred_element_type=F32)
    b_rows[...] = pick_s - select_left(pick_e, w)
    e_rows[...] = select_left(pick_e, einv[...])
    far(2, n_all)
    i0, i1 = (lax.broadcasted_iota(jnp.int32, (NS, NS), d) for d in (0, 1))
    t0, t1, t2 = n_all[:, :TILE], n_all[:, TILE : 3 * TILE], n_all[:, 3 * TILE :]
    normal[:TILE, :TILE] = t0
    normal[TILE:NE, :NE] = t1
    normal[NE:, :] = t2
    normal[:TILE, TILE:NE] = t1[:, :TILE].T
    normal[:TILE, NE:] = t2[:, :TILE].T
    normal[TILE:NE, NE:] = t2[:, TILE:NE].T
    normal[...] = normal[...] + jnp.where(i0 == i1, diag[...].reshape(1, NS), 0.0)
    for copy in sent:
        copy.wait_send()


def third_kernel(normal, sep, base, h, weights, b_rows, e_rows, out, rows, inverse):
    verified_inverse(normal, inverse, 0.25, 4)
    x = inverse[...]
    w = weights[...]
    out[...] = base[...] + fast(fast(h[...], x), h[...], ((1,), (1,)))
    t = fast(b_rows[...], x)
    rows[:, :NE] = e_rows[...] - fast(t, w, ((1,), (1,)))
    rows[:, NE:] = select_right(t, national(sep[...]))


def body(interior, coupling, tile_mask, prior, sep_map, nat_diag):
    count = prior.shape[1]
    sds = lambda *shape: jax.ShapeDtypeStruct(shape, F32)
    v = pl.BlockSpec(memory_space=VMEM)
    s = pl.BlockSpec(memory_space=pltpu.SMEM)
    dma = pltpu.SemaphoreType.DMA
    buf = lambda *shape: VMEM(shape, F32)
    ainv = pl.pallas_call(
        first_kernel,
        out_shape=sds(NI, NI),
        in_specs=[v],
        out_specs=v,
        compiler_params=pltpu.CompilerParams(vmem_limit_bytes=GRANT),
    )(interior[0, 0])
    normal, weights, base, h, b_rows, e_rows = pl.pallas_call(
        second_kernel,
        out_shape=(sds(NS, NS), sds(NE, NS), sds(NI, NI), sds(NI, NS), sds(count, NS), sds(count, NE)),
        in_specs=[s, v, v, v, v, v],
        out_specs=(v,) * 6,
        scratch_shapes=[
            buf(TILE, NS), buf(TILE, 2 * NS), buf(TILE, 2 * NS),
            buf(64, 2 * NS), buf(64, 2 * NS), buf(64, 2 * NS), buf(64, 2 * NS),
            buf(16, 8, NS), buf(8, 8, 2 * NS), buf(8, 8, 2 * NS),
            buf(TILE, NS), buf(TILE, 2 * NS), buf(4, 8, 2 * NS), buf(4, 8, 2 * NS), buf(TILE, 2 * NS),
            buf(NE, NE), buf(3, TILE, TILE),
            dma((16,)), dma((2,)), dma((2, 8)), dma((3, 16)), dma((2, 4)), dma((82,)),
        ],
        compiler_params=pltpu.CompilerParams(collective_id=0, has_side_effects=True, vmem_limit_bytes=GRANT),
    )(tile_mask[0], ainv, coupling[0, 0], prior[0], sep_map, nat_diag)
    result, rows = pl.pallas_call(
        third_kernel,
        out_shape=(sds(NI, NI), sds(count, NRC)),
        in_specs=[v] * 7,
        out_specs=(v, v),
        scratch_shapes=[buf(NS, NS)],
        compiler_params=pltpu.CompilerParams(vmem_limit_bytes=GRANT),
    )(normal, sep_map, base, h, weights, b_rows, e_rows)
    return (result[None, None], rows[None])


def solution(mesh):
    placed = (
        P("region", "dev", None, None),
        P("region", "dev", None, None),
        P("region", "dev", None),
        P("region", "dev", None),
        P("region", None),
        P(),
    )
    return jax.shard_map(
        body,
        mesh=mesh,
        in_specs=placed,
        out_specs=(P("region", "dev", None, None), P("region", "dev", None)),
        check_vma=False,
    )
```
